32 devices in a mesh: dp: 4 (over y, core), expert: 8 (over z, x).
Axes of the slice: x: 2, y: 2, z: 4, core: 2. Of those that a mesh axis runs over, the one named last changes fastest.
Arguments:
- tokens: bfloat16 [8, 16, 4096], P('expert', None, 'dp'), may hold values from -6 to 6
- routes: int32 [8, 16, 8], P('expert'), may hold values from 0 to 7, all different within a row; in each aligned block of 16 rows (0 to 15, 16 to 31, ..., all dimensions but the last counted through in order) at most 16 rows name the same one
- gates: float32 [8, 16, 8], P('expert'), may hold values from 0.05 to 0.3
- plan: int32 [8], replicated, may hold values from 0 to 7, each once
- proj_weight: bfloat16 [8, 2, 4096, 768], P('expert', None, 'dp'), may hold values from -0.09375 to 0.09375
- proj_grad: bfloat16 [8, 2, 4096, 768], P('expert', None, 'dp'), may hold values from -6 to 6
- first_moment: float32 [8, 2, 4096, 768], P('expert', None, 'dp'), may hold values from -1.8 to 1.8
- second_moment: float32 [8, 2, 4096, 768], P('expert', None, 'dp'), may hold values from 0.01 to 0.1
- down_weight: bfloat16 [8, 768, 4096], P('expert', None, 'dp'), may hold values from -0.21875 to 0.21875
Outputs:
- out_tokens: bfloat16 [8, 16, 4096], P('expert', None, 'dp')
- new_proj: bfloat16 [8, 2, 4096, 768], P('expert', None, 'dp')
- new_down: bfloat16 [8, 768, 4096], P('expert', None, 'dp')
The draws below stay inside these ranges and needn't reach their ends.
Inputs may be any that keep to these rules, and one draw needn't show every extreme that they name: `routes`: each token names 8 different experts; within one group no expert is named by more than 16 tokens, and in some group some expert is named by exactly 16. Expert x moves to the owner plan[x]; every owner receives exactly one expert.
All inputs are finite; a program needn't handle non-finite values.
Results may differ from the reference program's by a relative error of at most 0.024.
Values may be sent and summed in bfloat16 or wider, within the bound.
A program may use at most 64 MiB of HBM per device.

```python
import math
import jax
import jax.numpy as jnp
import numpy as np
from jax import lax

D = 4096
F = 768
TOPK = 8
GROUP_TOK = 16
GROUPS = 8
EXPERTS = 8
MOST = 16
N_DP = 4


def shard_levels(rng, shape, pieces, low, largest):
    factor_of = 1.0
    for axis_at, parts in pieces:
        heights = jax.random.uniform(jax.random.fold_in(jax.random.fold_in(rng, 6), axis_at), (parts,), jnp.float32, low / len(pieces), largest / len(pieces))
        factor_of = factor_of * jnp.repeat(jnp.exp(heights), shape[axis_at] // parts).reshape((-1,) + (1,) * (len(shape) - 1 - axis_at))
    return factor_of


def shared_out(stream_key, own, number, rows, amount, top, reach, skew):
    order = jax.random.permutation(stream_key, amount)
    packed, usual = shares(amount, rows * top, reach, skew, True), shares(amount, rows * top, reach, skew, False)
    places = jnp.arange(amount)

    def named(tallies, offset_by):
        used = int((tallies > 0).sum())
        fixed = max(1, used // 4)
        moved = fixed + (places - fixed + offset_by * (used - fixed)) % max(1, amount - fixed)
        return jnp.zeros((amount,), jnp.int32).at[order[jnp.where(places < fixed, places, moved)]].set(jnp.asarray(tallies, jnp.int32))

    tallies = jnp.where(number % 4 == 0, named(packed, number // 4), named(usual, number - number // 4 - 1))
    mixed = jax.random.permutation(jax.random.fold_in(own, 3), amount)
    source_of, receiver = mixed[0:amount // 2 * 2:2], mixed[1:amount // 2 * 2:2]
    slack = jnp.minimum(tallies[source_of] - 1, reach - tallies[receiver]) // 2
    slack = jnp.where((source_of == order[0]) | (receiver == order[0]) | (tallies[receiver] == 0), 0, jnp.maximum(slack, 0))
    moved = jax.random.randint(jax.random.fold_in(own, 4), (amount // 2,), 0, 1 << 20) % (slack + 1)
    tallies = tallies.at[source_of].add(-moved).at[receiver].add(moved)
    labels = jnp.searchsorted(jnp.cumsum(tallies), jnp.arange(rows * top), side="right").astype(jnp.int32)
    listing = labels.reshape(top, rows).T
    listing = listing[jax.random.permutation(jax.random.fold_in(own, 1), rows)]
    offset_by = jax.random.randint(jax.random.fold_in(own, 2), (rows, 1), 0, top)
    return jnp.take_along_axis(listing, (jnp.arange(top)[None, :] + offset_by) % top, axis=1)


def shares(count, total, limit, skew, full):
    loads = [(1 << 20) // math.isqrt(standing ** skew) + 1 for standing in range(1, count + 1)]
    largest = limit if full else min(limit, max(-(-total // count), total * loads[0] // sum(loads)))
    least = 1 if total - largest >= count - 1 else 0
    counts, rest = [largest] + [least] * (count - 1), total - largest - least * (count - 1)
    while rest > 0:
        candidates = [i for i in range(1, count) if counts[i] < largest] or [i for i in range(1, count) if counts[i] < limit]
        mass, remaining = sum([loads[i] for i in candidates]), rest
        for i in candidates:
            more = min(limit - counts[i], max(1, remaining * loads[i] // mass), rest)
            counts[i] = counts[i] + more
            rest = rest - more
    return np.array(counts)


def centred(stream_key, shape, width, bound, split=(), held_as=jnp.bfloat16):
    loudness = shard_levels(stream_key, shape, split, -0.22, 0.18) if split else 1.0
    values = jax.random.normal(stream_key, shape, jnp.float32) * width * loudness
    return jnp.minimum(jnp.maximum(values, -bound), bound).astype(held_as)


def setup_inputs(seed: int = 0) -> dict:
    key_list = jax.random.split(jax.random.key(seed), 10)
    tokens = centred(key_list[0], (GROUPS, GROUP_TOK, D), 1.0, 6.0, ((0, 8), (2, 4)))
    routes_keys = jax.random.split(jax.random.fold_in(key_list[1], 1), GROUPS * GROUP_TOK // GROUP_TOK)
    routes_turns = jax.random.permutation(jax.random.fold_in(key_list[1], 3), GROUPS * GROUP_TOK // GROUP_TOK)
    routes = jax.vmap(lambda own, number: shared_out(jax.random.fold_in(key_list[1], 2), own, number, GROUP_TOK, EXPERTS, TOPK, MOST, 2))(routes_keys, routes_turns).reshape((GROUPS, GROUP_TOK, TOPK))
    gates = jnp.clip(0.05 + 0.25 * jax.random.uniform(key_list[2], (GROUPS, GROUP_TOK, TOPK), jnp.float32) ** shard_levels(key_list[2], (GROUPS, GROUP_TOK, TOPK), ((0, 8),), -0.2, 0.2), 0.05, 0.3)
    plan = jax.random.permutation(key_list[3], EXPERTS).astype(jnp.int32)
    proj_weight = centred(key_list[4], (EXPERTS, 2, D, F), D ** -0.5, 0.09375, ((0, 8), (2, 4)))
    proj_grad = centred(key_list[5], (EXPERTS, 2, D, F), 1.0, 6.0, ((0, 8), (2, 4)))
    first_moment = centred(key_list[6], (EXPERTS, 2, D, F), 0.3, 1.8, ((0, 8), (2, 4)), jnp.float32)
    second_moment = jnp.clip(jnp.exp(math.log(0.1) - 2.3025851 * jax.random.uniform(key_list[7], (EXPERTS, 2, D, F), jnp.float32) ** shard_levels(key_list[7], (EXPERTS, 2, D, F), ((0, 8), (2, 4)), -0.2, 0.2)), 0.01, 0.1)
    down_weight = centred(key_list[8], (EXPERTS, F, D), F ** -0.5, 0.21875, ((0, 8), (2, 4)))
    return dict(tokens=tokens, routes=routes, gates=gates, plan=plan, proj_weight=proj_weight, proj_grad=proj_grad, first_moment=first_moment, second_moment=second_moment, down_weight=down_weight)


learning_rate = 0.01
beta_first = 0.9
beta_second = 0.999
adam_epsilon = 1e-08
bias_first = 1.0 - 0.9 ** 10
bias_second = 1.0 - 0.999 ** 10

def adam_update(weights, grads, first_moment, second_moment):
    grad_float = grads.astype(jnp.float32)
    first_new = beta_first * first_moment + (1.0 - beta_first) * grad_float
    second_new = beta_second * second_moment + (1.0 - beta_second) * grad_float * grad_float
    adam_step = first_new / bias_first / (jnp.sqrt(second_new / bias_second) + adam_epsilon)
    return (weights.astype(jnp.float32) - learning_rate * adam_step).astype(jnp.bfloat16)

def reference(tokens, routes, gates, plan, proj_weight, proj_grad, first_moment, second_moment, down_weight):
    updated = adam_update(proj_weight, proj_grad, first_moment, second_moment)
    new_proj = jnp.zeros_like(updated).at[plan].set(updated)
    new_down = jnp.zeros_like(down_weight).at[plan].set(down_weight)
    slot_ids = jnp.arange(MOST, dtype=jnp.int32)
    token_float = tokens.astype(jnp.float32)
    block_width = D // N_DP

    def one_expert(running, expert):
        matches = routes == expert
        routed = lax.optimization_barrier(jnp.sum(matches.astype(jnp.int32), axis=2))
        weighting = lax.optimization_barrier(jnp.sum(jnp.where(matches, gates, 0.0), axis=2))
        ranks = jnp.cumsum(routed, axis=1) - routed
        select = jnp.logical_and(ranks[:, None, :] == slot_ids[None, :, None], routed[:, None, :] > 0).astype(jnp.float32)
        slots = jnp.einsum('gst,gtd->gsd', select, token_float).astype(jnp.bfloat16).reshape(GROUPS * MOST, D)
        projection = updated[expert]
        joined = jnp.concatenate([projection[0], projection[1]], axis=1)
        slot_blocks = slots.reshape(GROUPS * MOST, N_DP, block_width).astype(jnp.float32)
        weight_blocks = joined.reshape(N_DP, block_width, 2 * F).astype(jnp.float32)
        partial_sums = jnp.einsum('snd,ndf->nsf', slot_blocks, weight_blocks)
        rounded = lax.optimization_barrier(partial_sums.astype(jnp.bfloat16))
        summed = lax.optimization_barrier(jnp.sum(rounded.astype(jnp.float32), axis=0))
        gate_act = summed[:, :F]
        up_act = summed[:, F:]
        hidden = (jax.nn.silu(gate_act) * up_act).astype(jnp.bfloat16)
        expert_out = jnp.dot(hidden, down_weight[expert], preferred_element_type=jnp.float32).astype(jnp.bfloat16)
        outputs = expert_out.reshape(GROUPS, MOST, D).astype(jnp.float32)
        running = running + jnp.einsum('gst,gsd->gtd', select * weighting[:, None, :], outputs)
        return (running, None)
    start_total = jnp.zeros((GROUPS, GROUP_TOK, D), jnp.float32)
    final_total, ignored = lax.scan(one_expert, start_total, jnp.arange(EXPERTS, dtype=jnp.int32))
    return (final_total.astype(jnp.bfloat16), new_proj, new_down)
```

```python
import functools

import jax
import jax.numpy as jnp
from jax import lax
from jax.experimental import pallas as pl
from jax.experimental.pallas import tpu as pltpu
from jax.sharding import PartitionSpec as P

learning_rate = 0.01
beta_first = 0.9
beta_second = 0.999
adam_epsilon = 1e-08
bias_first = 1.0 - 0.9**10
bias_second = 1.0 - 0.999**10

chunk_rows = 32
adam_rows = 64
adam_buffers = 4
skew = 2
lead = 8
lag = 2
token_steps = (17, 20, 23, 30)
max_levels = 4
vmem_limit = 60 * 2**20


def adam_update(weights, grads, first_moment, second_moment):
    grad_float = grads.astype(jnp.float32)
    first_new = beta_first * first_moment + (1.0 - beta_first) * grad_float
    second_new = beta_second * second_moment + (1.0 - beta_second) * grad_float * grad_float
    adam_step = first_new / bias_first / (jnp.sqrt(second_new / bias_second) + adam_epsilon)
    return (weights.astype(jnp.float32) - learning_rate * adam_step).astype(jnp.bfloat16)


def partial_products(slots, updated):
    joined = jnp.concatenate([updated[0], updated[1]], axis=1)
    return jnp.dot(slots, joined, preferred_element_type=jnp.float32).astype(jnp.bfloat16)


def dp_blocks(partials):
    parts = lax.axis_size("dp")
    return lax.all_to_all(
        partials.reshape(1, parts, -1, partials.shape[1]),
        "dp",
        split_axis=1,
        concat_axis=1,
        tiled=True,
    )


def finish_rows(blocks, down_local):
    width = down_local.shape[0]
    summed = jnp.sum(blocks[0].astype(jnp.float32), axis=0)
    hidden = (jax.nn.silu(summed[:, :width]) * summed[:, width:]).astype(jnp.bfloat16)
    result = jnp.dot(
        lax.all_gather(hidden, "dp", axis=0, tiled=True),
        down_local,
        preferred_element_type=jnp.float32,
    )
    return result.astype(jnp.bfloat16)


def owner_exchange(pieces):
    return lax.all_to_all(pieces, "expert", split_axis=1, concat_axis=1, tiled=True)


def two_phase_migration(plan, updated, down_local):
    owners = lax.axis_size("expert")
    local_rows, width = updated.shape[1:]
    expert_ids = jnp.arange(owners, dtype=jnp.int32)
    spread_down = owner_exchange(down_local.reshape(1, owners, width // owners, local_rows))
    spread_proj = owner_exchange(updated.reshape(2, owners, local_rows // owners, width))
    inverse = jnp.sum(
        jnp.where(plan[None, :] == expert_ids[:, None], expert_ids[None, :], 0), axis=1
    )

    def reordered(blocks):
        return jnp.concatenate(
            [lax.dynamic_slice_in_dim(blocks, inverse[e], 1, axis=1) for e in range(owners)], axis=1
        )

    moved_down = owner_exchange(reordered(spread_down))
    moved_proj = owner_exchange(reordered(spread_proj))
    return moved_proj.reshape(2, local_rows, width), moved_down.reshape(width, local_rows)


def generic_body(
    tokens, routes, gates, plan, proj_weight, proj_grad, first_moment, second_moment, down_weight
):
    owners = lax.axis_size("expert")
    local_rows = proj_weight.shape[2]
    group_tokens = tokens.shape[1]
    route_count = routes.shape[2]
    capacity = min(group_tokens, 3 * group_tokens * route_count // (2 * owners))
    down_local = down_weight[0]
    expert_ids = jnp.arange(owners, dtype=jnp.int32)
    target_match = routes[0][:, :, None] == expert_ids[None, None, :]
    routed = jnp.sum(target_match.astype(jnp.int32), axis=1)
    weighting = jnp.sum(jnp.where(target_match, gates[0][:, :, None], 0.0), axis=1)
    token_ids = jnp.arange(group_tokens, dtype=jnp.int32)
    before = (token_ids[None, :] < token_ids[:, None]).astype(jnp.bfloat16)
    ranks = jnp.dot(
        before, routed.astype(jnp.bfloat16), preferred_element_type=jnp.float32
    ).astype(jnp.int32)
    slot_ids = jnp.arange(capacity, dtype=jnp.int32)
    select = jnp.logical_and(
        ranks.T[:, None, :] == slot_ids[None, :, None], routed.T[:, None, :] > 0
    )
    dispatch_buf = jnp.einsum(
        "ost,td->osd", select.astype(jnp.bfloat16), tokens[0], preferred_element_type=jnp.float32
    ).astype(jnp.bfloat16)
    arrived = owner_exchange(dispatch_buf[None])
    slots = arrived.reshape(owners * capacity, local_rows)
    updated = adam_update(proj_weight[0], proj_grad[0], first_moment[0], second_moment[0])
    new_proj, new_down = two_phase_migration(plan, updated, down_local)
    expert_out = finish_rows(dp_blocks(partial_products(slots, updated)), down_local)
    returned = owner_exchange(expert_out.reshape(1, owners, capacity, local_rows))
    combine = select.astype(jnp.float32) * weighting.T[:, None, :]
    mixed = jnp.einsum(
        "ost,osd->td", combine, returned[0].astype(jnp.float32), precision=lax.Precision.HIGHEST
    )
    return (mixed.astype(jnp.bfloat16)[None], new_proj[None], new_down[None])


def foldable(local_rows, width):
    extra = local_rows - width
    return (
        extra > 0
        and width % extra == 0
        and (width // 2) % (width // extra) == 0
        and local_rows % adam_rows == 0
        and ((width // 2) * local_rows // width) % chunk_rows == 0
    )


def lane_slots(sources, targets, lanes, upward):
    count = len(sources)
    order = range(count) if upward else range(count - 1, -1, -1)
    lane_of, moves, done = {}, {}, []
    for e in order:
        moves[e] = targets[e] > sources[e] if upward else targets[e] < sources[e]
        lane = jnp.int32(0)
        found = jnp.bool_(False)
        for k in range(lanes):
            taken = jnp.bool_(False)
            for p in done:
                if upward:
                    open_still = targets[p] > sources[e]
                else:
                    open_still = targets[p] < sources[e]
                taken = taken | (moves[p] & open_still & (lane_of[p] == k))
            lane = jnp.where(jnp.logical_not(found) & jnp.logical_not(taken), k, lane)
            found = found | jnp.logical_not(taken)
        lane_of[e] = lane
        done.append(e)
    return lane_of, moves


def step_kernel(
    lanes,
    plan,
    routes,
    gates,
    tokens,
    weight_hbm,
    grad_hbm,
    first_hbm,
    second_hbm,
    down_hbm,
    out_tokens,
    new_proj,
    new_down,
    own,
    cross,
    stage_up,
    stage_down,
    got_up,
    got_down,
    stage_final,
    final,
    weight_buf,
    grad_buf,
    first_buf,
    second_buf,
    down_buf,
    slots,
    partial_out,
    partial_in,
    hidden,
    expert_out,
    returned,
    fold_sem,
    down_sem,
    adam_sem,
    cross_send,
    cross_recv,
    up_send,
    up_recv,
    down_send,
    down_recv,
    final_send,
    final_recv,
    write_sem,
    token_send,
    token_recv,
    partial_send,
    partial_recv,
    hidden_send,
    hidden_recv,
    return_send,
    return_recv,
):
    owners = lax.axis_size("expert")
    parts = lax.axis_size("dp")
    levels = owners // 2
    local_rows, width = weight_hbm.shape[2:]
    half_width = width // 2
    extra = local_rows - width
    strips = width // extra
    tall = half_width // strips
    folded = half_width * local_rows // width
    total = folded + local_rows
    chunks, down_chunks = total // chunk_rows, folded // chunk_rows
    blocks = local_rows // adam_rows
    group = tokens.shape[1]
    per_part = owners * group // parts
    me, my_part = lax.axis_index("expert"), lax.axis_index("dp")
    level, line = me // 2, me % 2
    partner = 2 * level + 1 - line

    def rows_of(c):
        return pl.ds(pl.multiple_of(c * chunk_rows, chunk_rows), chunk_rows)

    def peer(r):
        return lax.rem(me + r, owners)

    def part_peer(r):
        return lax.rem(my_part + r, parts)

    def fold_copies():
        made = []
        for h in (0, 1):
            made.append(
                pltpu.make_async_copy(
                    down_hbm.at[0, pl.ds(h * half_width, half_width), pl.ds(0, width)],
                    own.at[h, pl.ds(0, half_width), :],
                    fold_sem,
                )
            )
            for i in range(strips):
                made.append(
                    pltpu.make_async_copy(
                        down_hbm.at[0, pl.ds(h * half_width + i * tall, tall), pl.ds(width, extra)],
                        own.at[h, pl.ds(half_width, tall), pl.ds(i * extra, extra)],
                        fold_sem,
                    )
                )
        return made

    def unfold_copies():
        made = []
        for h in (0, 1):
            made.append(
                pltpu.make_async_copy(
                    final.at[h, pl.ds(0, half_width), :],
                    new_down.at[0, pl.ds(h * half_width, half_width), pl.ds(0, width)],
                    write_sem.at[0],
                )
            )
            for i in range(strips):
                made.append(
                    pltpu.make_async_copy(
                        final.at[h, pl.ds(half_width, tall), pl.ds(i * extra, extra)],
                        new_down.at[0, pl.ds(h * half_width + i * tall, tall), pl.ds(width, extra)],
                        write_sem.at[0],
                    )
                )
        return made

    def adam_copies(block):
        slot = lax.rem(block, adam_buffers)
        rows = pl.ds(pl.multiple_of(block * adam_rows, adam_rows), adam_rows)
        pairs = (
            (weight_hbm, weight_buf),
            (grad_hbm, grad_buf),
            (first_hbm, first_buf),
            (second_hbm, second_buf),
        )
        return [
            pltpu.make_async_copy(
                source.at[0, :, rows, :], target.at[slot], adam_sem.at[n, slot]
            )
            for n, (source, target) in enumerate(pairs)
        ]

    def cross_copy(c):
        return pltpu.make_async_remote_copy(
            src_ref=own.at[1 - line, rows_of(c), :],
            dst_ref=cross.at[rows_of(c), :],
            send_sem=cross_send,
            recv_sem=cross_recv.at[c],
            device_id={"expert": partner},
        )

    def up_copy(c, target):
        return pltpu.make_async_remote_copy(
            src_ref=stage_up.at[c],
            dst_ref=got_up.at[c],
            send_sem=up_send,
            recv_sem=up_recv.at[c],
            device_id={"expert": target},
        )

    def down_copy(c, target):
        return pltpu.make_async_remote_copy(
            src_ref=stage_down.at[c],
            dst_ref=got_down.at[c],
            send_sem=down_send,
            recv_sem=down_recv.at[c],
            device_id={"expert": target},
        )

    def final_copy(c, h):
        return pltpu.make_async_remote_copy(
            src_ref=stage_final.at[rows_of(c), :],
            dst_ref=final.at[h, rows_of(c), :],
            send_sem=final_send,
            recv_sem=final_recv.at[c],
            device_id={"expert": partner},
        )

    def token_copy(r, slot):
        return pltpu.make_async_remote_copy(
            src_ref=tokens.at[0],
            dst_ref=slots.at[slot],
            send_sem=token_send.at[r],
            recv_sem=token_recv.at[r],
            device_id={"expert": peer(r)},
        )

    def partial_copy(r, slot):
        return pltpu.make_async_remote_copy(
            src_ref=partial_out.at[part_peer(r)],
            dst_ref=partial_in.at[slot],
            send_sem=partial_send.at[r],
            recv_sem=partial_recv.at[r],
            device_id={"dp": part_peer(r)},
        )

    def hidden_copy(r, slot):
        return pltpu.make_async_remote_copy(
            src_ref=hidden.at[slot],
            dst_ref=hidden.at[slot],
            send_sem=hidden_send.at[r],
            recv_sem=hidden_recv.at[r],
            device_id={"dp": part_peer(r)},
        )

    def return_copy(r, slot):
        return pltpu.make_async_remote_copy(
            src_ref=expert_out.at[peer(r)],
            dst_ref=returned.at[slot],
            send_sem=return_send.at[r],
            recv_sem=return_recv.at[r],
            device_id={"expert": peer(r)},
        )

    for copy in fold_copies():
        copy.start()
    for block in range(adam_buffers):
        for copy in adam_copies(jnp.int32(block)):
            copy.start()
    down_load = pltpu.make_async_copy(down_hbm.at[0], down_buf, down_sem)
    down_load.start()

    barrier = pltpu.get_barrier_semaphore()
    for r in range(1, owners):
        pl.semaphore_signal(barrier, inc=1, device_id={"expert": peer(r)})
    for r in range(1, parts):
        pl.semaphore_signal(barrier, inc=1, device_id={"dp": part_peer(r)})
    pl.semaphore_wait(barrier, owners + parts - 2)

    for r in range(1, owners):
        token_copy(r, me).start()
    slots[me] = tokens[0]
    pltpu.make_async_copy(
        own.at[:, pl.ds(0, folded), :], own.at[:, pl.ds(0, folded), :], fold_sem
    ).wait()
    for c in range(lead):
        cross_copy(c).start()

    sources = [e // 2 for e in range(owners)]
    targets = [plan[e] // 2 for e in range(owners)]
    up_lane, goes_up = lane_slots(sources, targets, lanes, True)
    down_lane, goes_down = lane_slots(sources, targets, lanes, False)

    def at_me(values):
        mine, other = jnp.int32(-1), jnp.int32(-1)
        for e in range(owners):
            mine = jnp.where(me == e, values[e], mine)
            other = jnp.where(partner == e, values[e], other)
        return mine, other

    up_mine, up_other = at_me([jnp.where(goes_up[e], up_lane[e], -1) for e in range(owners)])
    down_mine, down_other = at_me(
        [jnp.where(goes_down[e], down_lane[e], -1) for e in range(owners)]
    )
    origin_mine, origin_other = jnp.int32(0), jnp.int32(0)
    for e in range(owners):
        origin = jnp.where(
            goes_up[e] & (level != sources[e]),
            2 + up_lane[e],
            jnp.where(
                goes_down[e] & (level != sources[e]),
                2 + lanes + down_lane[e],
                jnp.where(me == e, 0, 1),
            ),
        )
        origin_mine = jnp.where(plan[e] == me, origin, origin_mine)
        origin_other = jnp.where(plan[e] == partner, origin, origin_other)

    def forward(c, got, stage, lane_mine, lane_other):
        mine = own[line, rows_of(c), :]
        other = cross[rows_of(c), :]
        for k in range(lanes):
            value = jnp.where(lane_mine == k, mine, got[c, k])
            stage[c, k] = jnp.where(lane_other == k, other, value)

    def adam_block(i):
        for copy in adam_copies(i):
            copy.wait()
        slot = lax.rem(i, adam_buffers)
        strips_of = adam_rows // 16

        def strip(j, unused):
            h = j // strips_of
            at = pl.multiple_of((j % strips_of) * 16, 16)
            rows = pl.ds(at, 16)
            grad = grad_buf[slot, h, rows, :].astype(jnp.float32)
            first = beta_first * first_buf[slot, h, rows, :] + (1.0 - beta_first) * grad
            second = beta_second * second_buf[slot, h, rows, :] + (1.0 - beta_second) * grad * grad
            scaled = first * (learning_rate / bias_first)
            denominator = jnp.sqrt(second * (1.0 / bias_second)) + adam_epsilon
            value = weight_buf[slot, h, rows, :].astype(jnp.float32) - scaled / denominator
            start = pl.multiple_of(folded + i * adam_rows + at, 16)
            own[h, pl.ds(start, 16), :] = value.astype(jnp.bfloat16)
            return unused

        lax.fori_loop(0, 2 * strips_of, strip, 0)

        @pl.when(i + adam_buffers < blocks)
        def _():
            for copy in adam_copies(i + adam_buffers):
                copy.start()

    def send_partials():
        for r in range(1, owners):
            token_copy(r, lax.rem(me + owners - r, owners)).wait_recv()
        gathered = slots[...].reshape(owners * group, local_rows)
        for h in (0, 1):
            product = jnp.dot(
                gathered, own[h, pl.ds(folded, local_rows), :], preferred_element_type=jnp.float32
            )
            partial_out[:, :, pl.ds(h * width, width)] = product.astype(jnp.bfloat16).reshape(
                parts, per_part, width
            )
        for r in range(1, parts):
            partial_copy(r, my_part).start()
        partial_in[my_part] = partial_out[my_part]

    def send_hidden():
        for r in range(1, parts):
            partial_copy(r, lax.rem(my_part + parts - r, parts)).wait_recv()
        summed = partial_in[0].astype(jnp.float32)
        for p in range(1, parts):
            summed = summed + partial_in[p].astype(jnp.float32)
        gate, up = summed[:, :width], summed[:, width:]
        hidden[my_part] = (gate / (1.0 + jnp.exp(-gate)) * up).astype(jnp.bfloat16)
        for r in range(1, parts):
            hidden_copy(r, my_part).start()

    def send_results():
        for r in range(1, parts):
            hidden_copy(r, lax.rem(my_part + parts - r, parts)).wait_recv()
        down_load.wait()
        product = jnp.dot(
            hidden[...].reshape(owners * group, width),
            down_buf[...],
            preferred_element_type=jnp.float32,
        )
        expert_out[...] = product.astype(jnp.bfloat16).reshape(owners, group, local_rows)
        for r in range(1, owners):
            return_copy(r, me).start()
        returned[me] = expert_out[me]

    def mix_results():
        for r in range(1, owners):
            return_copy(r, lax.rem(me + owners - r, owners)).wait_recv()
        mixed = jnp.zeros((group, local_rows), jnp.float32)
        for e in range(owners):
            gate = jnp.sum(jnp.where(routes[0] == e, gates[0], 0.0), axis=1, keepdims=True)
            mixed = mixed + gate * returned[e].astype(jnp.float32)
        out_tokens[0] = mixed.astype(jnp.bfloat16)

    reach = (levels - 1) * skew

    def step(i, unused):
        @pl.when(i < blocks)
        def _():
            adam_block(i)

        @pl.when(i + lead < chunks)
        def _():
            cross_copy(i + lead).start()

        @pl.when(i < chunks)
        def _():
            cross_copy(i).wait_recv()

        up_at = i - level * skew

        @pl.when((up_at >= 0) & (up_at < chunks))
        def _():
            @pl.when(level > 0)
            def _():
                up_copy(up_at, me).wait_recv()

            @pl.when(level < levels - 1)
            def _():
                forward(up_at, got_up, stage_up, up_mine, up_other)
                up_copy(up_at, me + 2).start()

        down_at = i - (levels - 1 - level) * skew

        @pl.when((down_at >= 0) & (down_at < chunks))
        def _():
            @pl.when(level < levels - 1)
            def _():
                down_copy(down_at, me).wait_recv()

            @pl.when(level > 0)
            def _():
                forward(down_at, got_down, stage_down, down_mine, down_other)
                down_copy(down_at, me - 2).start()

        at = i - reach

        @pl.when((at >= 0) & (at < chunks))
        def _():
            mine = own[line, rows_of(at), :]
            other = cross[rows_of(at), :]
            keep = jnp.where(origin_mine == 0, mine, other)
            give = jnp.where(origin_other == 0, mine, other)
            for k in range(lanes):
                value = got_up[at, k]
                keep = jnp.where(origin_mine == 2 + k, value, keep)
                give = jnp.where(origin_other == 2 + k, value, give)
                value = got_down[at, k]
                keep = jnp.where(origin_mine == 2 + lanes + k, value, keep)
                give = jnp.where(origin_other == 2 + lanes + k, value, give)
            stage_final[rows_of(at), :] = give
            final_copy(at, line).start()
            final[line, rows_of(at), :] = keep

        landed = i - reach - lag

        @pl.when((landed >= 0) & (landed < chunks))
        def _():
            final_copy(landed, 1 - line).wait_recv()

            @pl.when(landed == down_chunks - 1)
            def _():
                for copy in unfold_copies():
                    copy.start()

            @pl.when(landed >= down_chunks)
            def _():
                out_rows = rows_of(landed - down_chunks)
                pltpu.make_async_copy(
                    final.at[:, rows_of(landed), :], new_proj.at[0, :, out_rows, :], write_sem.at[1]
                ).start()

        for when, work in zip(
            token_steps, (send_partials, send_hidden, send_results, mix_results)
        ):
            pl.when(i == when)(work)
        return unused

    lax.fori_loop(0, chunks + reach + lag, step, 0)

    for r in range(1, owners):
        token_copy(r, me).wait_send()
        return_copy(r, me).wait_send()
    for r in range(1, parts):
        partial_copy(r, my_part).wait_send()
        hidden_copy(r, my_part).wait_send()

    def whole_wait(buffer, sem):
        pltpu.make_async_remote_copy(
            src_ref=buffer, dst_ref=buffer, send_sem=sem, recv_sem=sem, device_id={"expert": partner}
        ).wait_send()

    whole_wait(cross, cross_send)
    whole_wait(stage_final, final_send)

    @pl.when(level < levels - 1)
    def _():
        whole_wait(stage_up, up_send)

    @pl.when(level > 0)
    def _():
        whole_wait(stage_down, down_send)

    done_down = final.at[:, pl.ds(0, folded), :]
    pltpu.make_async_copy(done_down, done_down, write_sem.at[0]).wait()
    done_proj = final.at[:, pl.ds(folded, local_rows), :]
    pltpu.make_async_copy(done_proj, done_proj, write_sem.at[1]).wait()


def step_call(lanes, tokens, routes, gates, plan, weights, grads, first, second, down):
    owners, parts = lax.axis_size("expert"), lax.axis_size("dp")
    local_rows, width = weights.shape[2:]
    group = tokens.shape[1]
    folded = (width // 2) * local_rows // width
    total = folded + local_rows
    chunks = total // chunk_rows
    per_part = owners * group // parts
    bf16, f32 = jnp.bfloat16, jnp.float32
    lane_buffer = pltpu.VMEM((chunks, lanes, chunk_rows, width), bf16)
    adam_shape = (adam_buffers, 2, adam_rows, width)
    dma = pltpu.SemaphoreType.DMA
    vmem = pl.BlockSpec(memory_space=pltpu.VMEM)
    hbm = pl.BlockSpec(memory_space=pl.ANY)
    moved = 2 * total * width * 2
    return pl.pallas_call(
        functools.partial(step_kernel, lanes),
        out_shape=(
            jax.ShapeDtypeStruct(tokens.shape, bf16),
            jax.ShapeDtypeStruct(weights.shape, bf16),
            jax.ShapeDtypeStruct(down.shape, bf16),
        ),
        in_specs=[pl.BlockSpec(memory_space=pltpu.SMEM), vmem, vmem, vmem] + [hbm] * 5,
        out_specs=(vmem, hbm, hbm),
        scratch_shapes=[
            pltpu.VMEM((2, total, width), bf16),
            pltpu.VMEM((total, width), bf16),
            lane_buffer,
            lane_buffer,
            lane_buffer,
            lane_buffer,
            pltpu.VMEM((total, width), bf16),
            pltpu.VMEM((2, total, width), bf16),
            pltpu.VMEM(adam_shape, bf16),
            pltpu.VMEM(adam_shape, bf16),
            pltpu.VMEM(adam_shape, f32),
            pltpu.VMEM(adam_shape, f32),
            pltpu.VMEM((width, local_rows), bf16),
            pltpu.VMEM((owners, group, local_rows), bf16),
            pltpu.VMEM((parts, per_part, 2 * width), bf16),
            pltpu.VMEM((parts, per_part, 2 * width), bf16),
            pltpu.VMEM((parts, per_part, width), bf16),
            pltpu.VMEM((owners, group, local_rows), bf16),
            pltpu.VMEM((owners, group, local_rows), bf16),
            dma,
            dma,
            dma((4, adam_buffers)),
            dma,
            dma((chunks,)),
            dma,
            dma((chunks,)),
            dma,
            dma((chunks,)),
            dma,
            dma((chunks,)),
            dma((2,)),
            dma((owners,)),
            dma((owners,)),
            dma((parts,)),
            dma((parts,)),
            dma((parts,)),
            dma((parts,)),
            dma((owners,)),
            dma((owners,)),
        ],
        compiler_params=pltpu.CompilerParams(
            collective_id=lanes, has_side_effects=True, vmem_limit_bytes=vmem_limit
        ),
        cost_estimate=pl.CostEstimate(
            flops=6 * owners * group * local_rows * width,
            bytes_accessed=6 * moved,
            transcendentals=2 * local_rows * width,
        ),
        name=f"adam_migrate_route_{lanes}",
    )(plan, routes, gates, tokens, weights, grads, first, second, down)


def body(
    tokens, routes, gates, plan, proj_weight, proj_grad, first_moment, second_moment, down_weight
):
    args = (tokens, routes, gates, plan, proj_weight, proj_grad, first_moment, second_moment, down_weight)
    owners = lax.axis_size("expert")
    levels = owners // 2
    if levels > max_levels or owners != routes.shape[2] or not foldable(*proj_weight.shape[2:]):
        return generic_body(*args)
    level_of = jnp.arange(owners, dtype=jnp.int32) // 2
    load = sum(
        jnp.where((level_of < cut) & (plan >= 2 * cut), 16**cut, 0) for cut in range(1, levels)
    )
    load = jnp.sum(load)
    widest = functools.reduce(
        jnp.maximum, [jnp.bitwise_and(load >> (4 * cut), 15) for cut in range(1, levels)]
    )
    choices = range(min(2, levels), levels + 1)
    return lax.switch(
        jnp.maximum(widest - choices[0], 0),
        [functools.partial(step_call, lanes) for lanes in choices],
        *args,
    )


def solution(mesh):
    in_specs = (
        P("expert", None, "dp"),
        P("expert", None, None),
        P("expert", None, None),
        P(),
        P("expert", None, "dp", None),
        P("expert", None, "dp", None),
        P("expert", None, "dp", None),
        P("expert", None, "dp", None),
        P("expert", None, "dp"),
    )
    out_specs = (P("expert", None, "dp"), P("expert", None, "dp", None), P("expert", None, "dp"))
    return jax.shard_map(body, mesh=mesh, in_specs=in_specs, out_specs=out_specs, check_vma=False)
```

```python
import functools

import jax
import jax.numpy as jnp
from jax import lax
from jax.experimental import pallas as pl
from jax.experimental.pallas import tpu as pltpu
from jax.sharding import PartitionSpec as P

learning_rate = 0.01
beta_first = 0.9
beta_second = 0.999
adam_epsilon = 1e-08
bias_first = 1.0 - 0.9**10
bias_second = 1.0 - 0.999**10

chunk_rows = 16
adam_rows = 64
adam_buffers = 4
skews = {1: 4, 2: 4, 3: 3, 4: 3}
lead = 14
lag = 5
token_steps = (4, 20, 30, 40)
return_step = 3
max_levels = 4
vmem_limit = {2: 38, 3: 48, 4: 54}


def adam_update(weights, grads, first_moment, second_moment):
    grad_float = grads.astype(jnp.float32)
    first_new = beta_first * first_moment + (1.0 - beta_first) * grad_float
    second_new = beta_second * second_moment + (1.0 - beta_second) * grad_float * grad_float
    adam_step = first_new / bias_first / (jnp.sqrt(second_new / bias_second) + adam_epsilon)
    return (weights.astype(jnp.float32) - learning_rate * adam_step).astype(jnp.bfloat16)


def partial_products(slots, updated):
    joined = jnp.concatenate([updated[0], updated[1]], axis=1)
    return jnp.dot(slots, joined, preferred_element_type=jnp.float32).astype(jnp.bfloat16)


def dp_blocks(partials):
    parts = lax.axis_size("dp")
    return lax.all_to_all(
        partials.reshape(1, parts, -1, partials.shape[1]),
        "dp",
        split_axis=1,
        concat_axis=1,
        tiled=True,
    )


def finish_rows(blocks, down_local):
    width = down_local.shape[0]
    summed = jnp.sum(blocks[0].astype(jnp.float32), axis=0)
    hidden = (jax.nn.silu(summed[:, :width]) * summed[:, width:]).astype(jnp.bfloat16)
    result = jnp.dot(
        lax.all_gather(hidden, "dp", axis=0, tiled=True),
        down_local,
        preferred_element_type=jnp.float32,
    )
    return result.astype(jnp.bfloat16)


def owner_exchange(pieces):
    return lax.all_to_all(pieces, "expert", split_axis=1, concat_axis=1, tiled=True)


def two_phase_migration(plan, updated, down_local):
    owners = lax.axis_size("expert")
    local_rows, width = updated.shape[1:]
    expert_ids = jnp.arange(owners, dtype=jnp.int32)
    spread_down = owner_exchange(down_local.reshape(1, owners, width // owners, local_rows))
    spread_proj = owner_exchange(updated.reshape(2, owners, local_rows // owners, width))
    inverse = jnp.sum(
        jnp.where(plan[None, :] == expert_ids[:, None], expert_ids[None, :], 0), axis=1
    )

    def reordered(blocks):
        return jnp.concatenate(
            [lax.dynamic_slice_in_dim(blocks, inverse[e], 1, axis=1) for e in range(owners)], axis=1
        )

    moved_down = owner_exchange(reordered(spread_down))
    moved_proj = owner_exchange(reordered(spread_proj))
    return moved_proj.reshape(2, local_rows, width), moved_down.reshape(width, local_rows)


def generic_body(
    tokens, routes, gates, plan, proj_weight, proj_grad, first_moment, second_moment, down_weight
):
    owners = lax.axis_size("expert")
    local_rows = proj_weight.shape[2]
    group_tokens = tokens.shape[1]
    route_count = routes.shape[2]
    capacity = min(group_tokens, 3 * group_tokens * route_count // (2 * owners))
    down_local = down_weight[0]
    expert_ids = jnp.arange(owners, dtype=jnp.int32)
    target_match = routes[0][:, :, None] == expert_ids[None, None, :]
    routed = jnp.sum(target_match.astype(jnp.int32), axis=1)
    weighting = jnp.sum(jnp.where(target_match, gates[0][:, :, None], 0.0), axis=1)
    token_ids = jnp.arange(group_tokens, dtype=jnp.int32)
    before = (token_ids[None, :] < token_ids[:, None]).astype(jnp.bfloat16)
    ranks = jnp.dot(
        before, routed.astype(jnp.bfloat16), preferred_element_type=jnp.float32
    ).astype(jnp.int32)
    slot_ids = jnp.arange(capacity, dtype=jnp.int32)
    select = jnp.logical_and(
        ranks.T[:, None, :] == slot_ids[None, :, None], routed.T[:, None, :] > 0
    )
    dispatch_buf = jnp.einsum(
        "ost,td->osd", select.astype(jnp.bfloat16), tokens[0], preferred_element_type=jnp.float32
    ).astype(jnp.bfloat16)
    arrived = owner_exchange(dispatch_buf[None])
    slots = arrived.reshape(owners * capacity, local_rows)
    updated = adam_update(proj_weight[0], proj_grad[0], first_moment[0], second_moment[0])
    new_proj, new_down = two_phase_migration(plan, updated, down_local)
    expert_out = finish_rows(dp_blocks(partial_products(slots, updated)), down_local)
    returned = owner_exchange(expert_out.reshape(1, owners, capacity, local_rows))
    combine = select.astype(jnp.float32) * weighting.T[:, None, :]
    mixed = jnp.einsum(
        "ost,osd->td", combine, returned[0].astype(jnp.float32), precision=lax.Precision.HIGHEST
    )
    return (mixed.astype(jnp.bfloat16)[None], new_proj[None], new_down[None])


def foldable(local_rows, width):
    extra = local_rows - width
    return (
        extra > 0
        and width % extra == 0
        and (width // 2) % (width // extra) == 0
        and local_rows % adam_rows == 0
        and ((width // 2) * local_rows // width) % chunk_rows == 0
    )


def lane_slots(sources, targets, lanes, upward):
    count = len(sources)
    order = range(count) if upward else range(count - 1, -1, -1)
    lane_of, moves, done = {}, {}, []
    for e in order:
        moves[e] = targets[e] > sources[e] if upward else targets[e] < sources[e]
        lane = jnp.int32(0)
        found = jnp.bool_(False)
        for k in range(lanes):
            taken = jnp.bool_(False)
            for p in done:
                if upward:
                    open_still = targets[p] > sources[e]
                else:
                    open_still = targets[p] < sources[e]
                taken = taken | (moves[p] & open_still & (lane_of[p] == k))
            lane = jnp.where(jnp.logical_not(found) & jnp.logical_not(taken), k, lane)
            found = found | jnp.logical_not(taken)
        lane_of[e] = lane
        done.append(e)
    return lane_of, moves


def step_kernel(
    lanes,
    plan,
    routes,
    gates,
    tokens,
    weight_hbm,
    grad_hbm,
    first_hbm,
    second_hbm,
    down_hbm,
    out_tokens,
    final,
    own,
    cross,
    stage_up,
    stage_down,
    got_up,
    got_down,
    stage_final,
    weight_buf,
    grad_buf,
    first_buf,
    second_buf,
    down_buf,
    slots,
    partial_out,
    partial_in,
    hidden,
    expert_out,
    returned,
    fold_sem,
    down_sem,
    adam_sem,
    cross_send,
    cross_recv,
    up_send,
    up_recv,
    down_send,
    down_recv,
    final_send,
    final_recv,
    token_send,
    token_recv,
    partial_send,
    partial_recv,
    hidden_send,
    hidden_recv,
    return_send,
    return_recv,
):
    owners = lax.axis_size("expert")
    parts = lax.axis_size("dp")
    levels = owners // 2
    local_rows, width = weight_hbm.shape[2:]
    half_width = width // 2
    extra = local_rows - width
    strips = width // extra
    tall = half_width // strips
    folded = half_width * local_rows // width
    total = folded + local_rows
    chunks, down_chunks = total // chunk_rows, folded // chunk_rows
    blocks = local_rows // adam_rows
    group = tokens.shape[1]
    per_part = owners * group // parts
    me, my_part = lax.axis_index("expert"), lax.axis_index("dp")
    level, line = me // 2, me % 2
    partner = 2 * level + 1 - line

    def rows_of(c):
        return pl.ds(pl.multiple_of(c * chunk_rows, chunk_rows), chunk_rows)

    def peer(r):
        return lax.rem(me + r, owners)

    def part_peer(r):
        return lax.rem(my_part + r, parts)

    def fold_copies():
        made = []
        for h in (0, 1):
            made.append(
                pltpu.make_async_copy(
                    down_hbm.at[0, pl.ds(h * half_width, half_width), pl.ds(0, width)],
                    own.at[h, pl.ds(0, half_width), :],
                    fold_sem,
                )
            )
            for i in range(strips):
                made.append(
                    pltpu.make_async_copy(
                        down_hbm.at[0, pl.ds(h * half_width + i * tall, tall), pl.ds(width, extra)],
                        own.at[h, pl.ds(half_width, tall), pl.ds(i * extra, extra)],
                        fold_sem,
                    )
                )
        return made

    def adam_copies(block):
        slot = lax.rem(block, adam_buffers)
        rows = pl.ds(pl.multiple_of(block * adam_rows, adam_rows), adam_rows)
        pairs = (
            (weight_hbm, weight_buf),
            (grad_hbm, grad_buf),
            (first_hbm, first_buf),
            (second_hbm, second_buf),
        )
        return [
            pltpu.make_async_copy(
                source.at[0, :, rows, :], target.at[slot], adam_sem.at[n, slot]
            )
            for n, (source, target) in enumerate(pairs)
        ]

    def cross_copy(c):
        return pltpu.make_async_remote_copy(
            src_ref=own.at[1 - line, rows_of(c), :],
            dst_ref=cross.at[rows_of(c), :],
            send_sem=cross_send,
            recv_sem=cross_recv.at[c],
            device_id={"expert": partner},
        )

    def up_copy(c, target):
        return pltpu.make_async_remote_copy(
            src_ref=stage_up.at[c],
            dst_ref=got_up.at[c],
            send_sem=up_send,
            recv_sem=up_recv.at[c],
            device_id={"expert": target},
        )

    def down_copy(c, target):
        return pltpu.make_async_remote_copy(
            src_ref=stage_down.at[c],
            dst_ref=got_down.at[c],
            send_sem=down_send,
            recv_sem=down_recv.at[c],
            device_id={"expert": target},
        )

    def final_copy(c, h):
        return pltpu.make_async_remote_copy(
            src_ref=stage_final.at[rows_of(c), :],
            dst_ref=final.at[h, rows_of(c), :],
            send_sem=final_send,
            recv_sem=final_recv.at[c],
            device_id={"expert": partner},
        )

    def token_copy(relayed, d, slot):
        target = 2 * lax.rem(level + d, levels) + line if d else partner
        return pltpu.make_async_remote_copy(
            src_ref=slots.at[slot],
            dst_ref=slots.at[slot],
            send_sem=token_send.at[relayed * levels + d],
            recv_sem=token_recv.at[relayed * levels + d],
            device_id={"expert": target},
        )

    def partial_copy(r, slot):
        return pltpu.make_async_remote_copy(
            src_ref=partial_out.at[part_peer(r)],
            dst_ref=partial_in.at[slot],
            send_sem=partial_send.at[r],
            recv_sem=partial_recv.at[r],
            device_id={"dp": part_peer(r)},
        )

    def hidden_copy(r, slot):
        return pltpu.make_async_remote_copy(
            src_ref=hidden.at[slot],
            dst_ref=hidden.at[slot],
            send_sem=hidden_send.at[r],
            recv_sem=hidden_recv.at[r],
            device_id={"dp": part_peer(r)},
        )

    def return_copy(r, slot):
        return pltpu.make_async_remote_copy(
            src_ref=expert_out.at[peer(r)],
            dst_ref=returned.at[slot],
            send_sem=return_send.at[r],
            recv_sem=return_recv.at[r],
            device_id={"expert": peer(r)},
        )

    for copy in fold_copies():
        copy.start()
    for block in range(adam_buffers):
        for copy in adam_copies(jnp.int32(block)):
            copy.start()
    down_load = pltpu.make_async_copy(down_hbm.at[0], down_buf, down_sem)
    down_load.start()

    barrier = pltpu.get_barrier_semaphore()
    for r in range(1, owners):
        pl.semaphore_signal(barrier, inc=1, device_id={"expert": peer(r)})
    for r in range(1, parts):
        pl.semaphore_signal(barrier, inc=1, device_id={"dp": part_peer(r)})
    pl.semaphore_wait(barrier, owners + parts - 2)

    slots[me] = tokens[0]
    pltpu.make_async_copy(
        own.at[:, pl.ds(0, folded), :], own.at[:, pl.ds(0, folded), :], fold_sem
    ).wait()
    for c in range(lead):
        cross_copy(c).start()
        if c == 0:
            for d in range(levels):
                token_copy(0, d, me).start()

    sources = [e // 2 for e in range(owners)]
    targets = [plan[e] // 2 for e in range(owners)]
    up_lane, goes_up = lane_slots(sources, targets, lanes, True)
    down_lane, goes_down = lane_slots(sources, targets, lanes, False)

    def at_me(values):
        mine, other = jnp.int32(-1), jnp.int32(-1)
        for e in range(owners):
            mine = jnp.where(me == e, values[e], mine)
            other = jnp.where(partner == e, values[e], other)
        return mine, other

    up_mine, up_other = at_me([jnp.where(goes_up[e], up_lane[e], -1) for e in range(owners)])
    down_mine, down_other = at_me(
        [jnp.where(goes_down[e], down_lane[e], -1) for e in range(owners)]
    )
    origin_mine, origin_other = jnp.int32(0), jnp.int32(0)
    for e in range(owners):
        origin = jnp.where(
            goes_up[e] & (level != sources[e]),
            2 + up_lane[e],
            jnp.where(
                goes_down[e] & (level != sources[e]),
                2 + lanes + down_lane[e],
                jnp.where(me == e, 0, 1),
            ),
        )
        origin_mine = jnp.where(plan[e] == me, origin, origin_mine)
        origin_other = jnp.where(plan[e] == partner, origin, origin_other)

    def forward(c, got, stage, lane_mine, lane_other):
        mine = own[line, rows_of(c), :]
        other = cross[rows_of(c), :]
        for k in range(lanes):
            value = jnp.where(lane_mine == k, mine, got[c, k])
            stage[c, k] = jnp.where(lane_other == k, other, value)

    def adam_block(i):
        for copy in adam_copies(i):
            copy.wait()
        slot = lax.rem(i, adam_buffers)
        strips_of = adam_rows // 16

        def strip(j, unused):
            h = j // strips_of
            at = pl.multiple_of((j % strips_of) * 16, 16)
            rows = pl.ds(at, 16)
            grad = grad_buf[slot, h, rows, :].astype(jnp.float32)
            first = beta_first * first_buf[slot, h, rows, :] + (1.0 - beta_first) * grad
            second = beta_second * second_buf[slot, h, rows, :] + (1.0 - beta_second) * grad * grad
            scaled = first * (learning_rate / bias_first)
            denominator = jnp.sqrt(second * (1.0 / bias_second)) + adam_epsilon
            value = weight_buf[slot, h, rows, :].astype(jnp.float32) - scaled / denominator
            start = pl.multiple_of(folded + i * adam_rows + at, 16)
            own[h, pl.ds(start, 16), :] = value.astype(jnp.bfloat16)
            return unused

        lax.fori_loop(0, 2 * strips_of, strip, 0)

        @pl.when(i + adam_buffers < blocks)
        def _():
            for copy in adam_copies(i + adam_buffers):
                copy.start()

    def relay_tokens():
        token_copy(0, 0, partner).wait_recv()
        for d in range(1, levels):
            token_copy(1, d, partner).start()

    def send_partials():
        for relayed in (0, 1):
            for d in range(1, levels):
                token_copy(relayed, d, me).wait_recv()
        gathered = slots[...].reshape(owners * group, local_rows)
        for h in (0, 1):
            product = jnp.dot(
                gathered, own[h, pl.ds(folded, local_rows), :], preferred_element_type=jnp.float32
            )
            partial_out[:, :, pl.ds(h * width, width)] = product.astype(jnp.bfloat16).reshape(
                parts, per_part, width
            )
        for r in range(1, parts):
            partial_copy(r, my_part).start()
        partial_in[my_part] = partial_out[my_part]

    def send_hidden():
        for r in range(1, parts):
            partial_copy(r, lax.rem(my_part + parts - r, parts)).wait_recv()
        summed = partial_in[0].astype(jnp.float32)
        for p in range(1, parts):
            summed = summed + partial_in[p].astype(jnp.float32)
        gate, up = summed[:, :width], summed[:, width:]
        hidden[my_part] = (gate / (1.0 + jnp.exp(-gate)) * up).astype(jnp.bfloat16)
        for r in range(1, parts):
            hidden_copy(r, my_part).start()

    def make_results():
        for r in range(1, parts):
            hidden_copy(r, lax.rem(my_part + parts - r, parts)).wait_recv()
        down_load.wait()
        product = jnp.dot(
            hidden[...].reshape(owners * group, width),
            down_buf[...],
            preferred_element_type=jnp.float32,
        )
        expert_out[...] = product.astype(jnp.bfloat16).reshape(owners, group, local_rows)

    def send_results():
        for r in range(1, owners):
            return_copy(r, me).start()
        returned[me] = expert_out[me]

    def mix_results():
        for r in range(1, owners):
            return_copy(r, lax.rem(me + owners - r, owners)).wait_recv()
        mixed = jnp.zeros((group, local_rows), jnp.float32)
        square = (group, group)
        same = lax.broadcasted_iota(jnp.int32, square, 0) == lax.broadcasted_iota(
            jnp.int32, square, 1
        )
        for e in range(owners):
            row = jnp.sum(jnp.where(routes[0] == e, gates[0], 0.0), axis=0, keepdims=True)
            gate = jnp.sum(jnp.where(same, row, 0.0), axis=1, keepdims=True)
            mixed = mixed + gate * returned[e].astype(jnp.float32)
        out_tokens[0] = mixed.astype(jnp.bfloat16)

    skew = skews[lanes]
    reach = (levels - 1) * skew

    def step(i, unused):
        @pl.when(i + lead < chunks)
        def _():
            cross_copy(i + lead).start()

        @pl.when(i < chunks)
        def _():
            cross_copy(i).wait_recv()

        up_at = i - level * skew

        @pl.when((up_at >= 0) & (up_at < chunks))
        def _():
            @pl.when(level > 0)
            def _():
                up_copy(up_at, me).wait_recv()

            @pl.when(level < levels - 1)
            def _():
                forward(up_at, got_up, stage_up, up_mine, up_other)
                up_copy(up_at, me + 2).start()

        down_at = i - (levels - 1 - level) * skew

        @pl.when((down_at >= 0) & (down_at < chunks))
        def _():
            @pl.when(level < levels - 1)
            def _():
                down_copy(down_at, me).wait_recv()

            @pl.when(level > 0)
            def _():
                forward(down_at, got_down, stage_down, down_mine, down_other)
                down_copy(down_at, me - 2).start()

        at = i - reach

        @pl.when((at >= 0) & (at < chunks))
        def _():
            mine = own[line, rows_of(at), :]
            other = cross[rows_of(at), :]
            keep = jnp.where(origin_mine == 0, mine, other)
            give = jnp.where(origin_other == 0, mine, other)
            for k in range(lanes):
                value = got_up[at, k]
                keep = jnp.where(origin_mine == 2 + k, value, keep)
                give = jnp.where(origin_other == 2 + k, value, give)
                value = got_down[at, k]
                keep = jnp.where(origin_mine == 2 + lanes + k, value, keep)
                give = jnp.where(origin_other == 2 + lanes + k, value, give)
            stage_final[rows_of(at), :] = give
            final_copy(at, line).start()
            final[line, rows_of(at), :] = keep

        landed = i - reach - lag

        @pl.when((landed >= 0) & (landed < chunks))
        def _():
            final_copy(landed, 1 - line).wait_recv()

        @pl.when(i < blocks)
        def _():
            adam_block(i)

        work = (relay_tokens, send_partials, send_hidden, make_results, send_results)
        for when, job in zip(token_steps + (chunks + skew + return_step,), work):
            pl.when(i == when)(job)
        return unused

    lax.fori_loop(0, chunks + reach + lag, step, 0)
    mix_results()

    for d in range(levels):
        token_copy(0, d, me).wait_send()
        if d:
            token_copy(1, d, partner).wait_send()
    for r in range(1, owners):
        return_copy(r, me).wait_send()
    for r in range(1, parts):
        partial_copy(r, my_part).wait_send()
        hidden_copy(r, my_part).wait_send()

    def whole_wait(buffer, sem):
        pltpu.make_async_remote_copy(
            src_ref=buffer, dst_ref=buffer, send_sem=sem, recv_sem=sem, device_id={"expert": partner}
        ).wait_send()

    whole_wait(cross, cross_send)
    whole_wait(stage_final, final_send)

    @pl.when(level < levels - 1)
    def _():
        whole_wait(stage_up, up_send)

    @pl.when(level > 0)
    def _():
        whole_wait(stage_down, down_send)


def write_kernel(tokens, final, out_tokens, new_proj, new_down, sem):
    local_rows, width = new_proj.shape[2:]
    half_width = width // 2
    extra = local_rows - width
    tall = half_width // (width // extra)
    folded = final.shape[1] - local_rows
    copies = [(tokens, out_tokens)]
    for h in (0, 1):
        copies.append((final.at[h, pl.ds(folded, local_rows), :], new_proj.at[0, h]))
        rows = pl.ds(h * half_width, half_width)
        copies.append((final.at[h, pl.ds(0, half_width), :], new_down.at[0, rows, pl.ds(0, width)]))
        for i in range(width // extra):
            rows = pl.ds(h * half_width + i * tall, tall)
            copies.append(
                (
                    final.at[h, pl.ds(half_width, tall), pl.ds(i * extra, extra)],
                    new_down.at[0, rows, pl.ds(width, extra)],
                )
            )
    made = [pltpu.make_async_copy(a, b, sem.at[n]) for n, (a, b) in enumerate(copies)]
    for copy in made:
        copy.start()
    for copy in made:
        copy.wait()


def write_call(tokens, final, weights, down):
    copies = 3 + 2 * (1 + down.shape[1] // (down.shape[2] - down.shape[1]))
    hbm = pl.BlockSpec(memory_space=pl.ANY)
    return pl.pallas_call(
        write_kernel,
        out_shape=[jax.ShapeDtypeStruct(a.shape, a.dtype) for a in (tokens, weights, down)],
        in_specs=[hbm, hbm],
        out_specs=[hbm, hbm, hbm],
        scratch_shapes=[pltpu.SemaphoreType.DMA((copies,))],
        compiler_params=pltpu.CompilerParams(vmem_limit_bytes=2**20),
        cost_estimate=pl.CostEstimate(
            flops=0, bytes_accessed=4 * final.size + 4 * tokens.size, transcendentals=0
        ),
        name="write_results",
    )(tokens, final)


def step_call(lanes, tokens, routes, gates, plan, weights, grads, first, second, down):
    owners, parts = lax.axis_size("expert"), lax.axis_size("dp")
    local_rows, width = weights.shape[2:]
    group = tokens.shape[1]
    folded = (width // 2) * local_rows // width
    total = folded + local_rows
    chunks = total // chunk_rows
    per_part = owners * group // parts
    bf16, f32 = jnp.bfloat16, jnp.float32
    lane_buffer = pltpu.VMEM((chunks, lanes, chunk_rows, width), bf16)
    adam_shape = (adam_buffers, 2, adam_rows, width)
    dma = pltpu.SemaphoreType.DMA
    vmem = pl.BlockSpec(memory_space=pltpu.VMEM)
    hbm = pl.BlockSpec(memory_space=pl.ANY)
    moved = 2 * total * width * 2
    return pl.pallas_call(
        functools.partial(step_kernel, lanes),
        out_shape=(
            jax.ShapeDtypeStruct(tokens.shape, bf16),
            pltpu.VMEM((2, total, width), bf16),
        ),
        in_specs=[pl.BlockSpec(memory_space=pltpu.SMEM), vmem, vmem, vmem] + [hbm] * 5,
        out_specs=(vmem, vmem),
        scratch_shapes=[
            pltpu.VMEM((2, total, width), bf16),
            pltpu.VMEM((total, width), bf16),
            lane_buffer,
            lane_buffer,
            lane_buffer,
            lane_buffer,
            pltpu.VMEM((total, width), bf16),
            pltpu.VMEM(adam_shape, bf16),
            pltpu.VMEM(adam_shape, bf16),
            pltpu.VMEM(adam_shape, f32),
            pltpu.VMEM(adam_shape, f32),
            pltpu.VMEM((width, local_rows), bf16),
            pltpu.VMEM((owners, group, local_rows), bf16),
            pltpu.VMEM((parts, per_part, 2 * width), bf16),
            pltpu.VMEM((parts, per_part, 2 * width), bf16),
            pltpu.VMEM((parts, per_part, width), bf16),
            pltpu.VMEM((owners, group, local_rows), bf16),
            pltpu.VMEM((owners, group, local_rows), bf16),
            dma,
            dma,
            dma((4, adam_buffers)),
            dma,
            dma((chunks,)),
            dma,
            dma((chunks,)),
            dma,
            dma((chunks,)),
            dma,
            dma((chunks,)),
            dma((owners,)),
            dma((owners,)),
            dma((parts,)),
            dma((parts,)),
            dma((parts,)),
            dma((parts,)),
            dma((owners,)),
            dma((owners,)),
        ],
        compiler_params=pltpu.CompilerParams(
            collective_id=lanes, has_side_effects=True, vmem_limit_bytes=vmem_limit[lanes] * 2**20
        ),
        cost_estimate=pl.CostEstimate(
            flops=6 * owners * group * local_rows * width,
            bytes_accessed=6 * moved,
            transcendentals=2 * local_rows * width,
        ),
        name=f"adam_migrate_route_{lanes}",
    )(plan, jnp.swapaxes(routes, 1, 2), jnp.swapaxes(gates, 1, 2), tokens, weights, grads, first, second, down)


def body(
    tokens, routes, gates, plan, proj_weight, proj_grad, first_moment, second_moment, down_weight
):
    args = (tokens, routes, gates, plan, proj_weight, proj_grad, first_moment, second_moment, down_weight)
    owners = lax.axis_size("expert")
    levels = owners // 2
    if levels > max_levels or owners != routes.shape[2] or not foldable(*proj_weight.shape[2:]):
        return generic_body(*args)
    fewest = min(2, levels)
    choices = range(fewest, levels + 1)
    expert_ids = jnp.arange(owners, dtype=jnp.int32)
    crossing = [
        jnp.sum(((expert_ids < 2 * cut) & (plan >= 2 * cut)).astype(jnp.int32))
        for cut in range(2, levels - 1)
    ]
    widest = functools.reduce(jnp.maximum, crossing, jnp.int32(fewest))

    def step_with(lanes):
        return lambda *args: write_call(*step_call(lanes, *args), proj_weight, down_weight)

    return lax.switch(widest - fewest, [step_with(lanes) for lanes in choices], *args)


def solution(mesh):
    in_specs = (
        P("expert", None, "dp"),
        P("expert", None, None),
        P("expert", None, None),
        P(),
        P("expert", None, "dp", None),
        P("expert", None, "dp", None),
        P("expert", None, "dp", None),
        P("expert", None, "dp", None),
        P("expert", None, "dp"),
    )
    out_specs = (P("expert", None, "dp"), P("expert", None, "dp", None), P("expert", None, "dp"))
    return jax.shard_map(body, mesh=mesh, in_specs=in_specs, out_specs=out_specs, check_vma=False)
```

```python
import functools

import jax
import jax.numpy as jnp
from jax import lax
from jax.experimental import pallas as pl
from jax.experimental.pallas import tpu as pltpu
from jax.sharding import PartitionSpec as P

learning_rate = 0.01
beta_first = 0.9
beta_second = 0.999
adam_epsilon = 1e-08
bias_first = 1.0 - 0.9**10
bias_second = 1.0 - 0.999**10

chunk_rows = 16
adam_rows = 64
adam_buffers = 4
skews = {1: 4, 2: 4, 3: 3, 4: 3}
lead = 14
lag = 5
pass_from = 0
pass_every = 3
token_steps = (20, 30, 40)
return_step = 3
max_levels = 4
vmem_limit = {2: 38, 3: 48, 4: 54}


def adam_update(weights, grads, first_moment, second_moment):
    grad_float = grads.astype(jnp.float32)
    first_new = beta_first * first_moment + (1.0 - beta_first) * grad_float
    second_new = beta_second * second_moment + (1.0 - beta_second) * grad_float * grad_float
    adam_step = first_new / bias_first / (jnp.sqrt(second_new / bias_second) + adam_epsilon)
    return (weights.astype(jnp.float32) - learning_rate * adam_step).astype(jnp.bfloat16)


def partial_products(slots, updated):
    joined = jnp.concatenate([updated[0], updated[1]], axis=1)
    return jnp.dot(slots, joined, preferred_element_type=jnp.float32).astype(jnp.bfloat16)


def dp_blocks(partials):
    parts = lax.axis_size("dp")
    return lax.all_to_all(
        partials.reshape(1, parts, -1, partials.shape[1]),
        "dp",
        split_axis=1,
        concat_axis=1,
        tiled=True,
    )


def finish_rows(blocks, down_local):
    width = down_local.shape[0]
    summed = jnp.sum(blocks[0].astype(jnp.float32), axis=0)
    hidden = (jax.nn.silu(summed[:, :width]) * summed[:, width:]).astype(jnp.bfloat16)
    result = jnp.dot(
        lax.all_gather(hidden, "dp", axis=0, tiled=True),
        down_local,
        preferred_element_type=jnp.float32,
    )
    return result.astype(jnp.bfloat16)


def owner_exchange(pieces):
    return lax.all_to_all(pieces, "expert", split_axis=1, concat_axis=1, tiled=True)


def two_phase_migration(plan, updated, down_local):
    owners = lax.axis_size("expert")
    local_rows, width = updated.shape[1:]
    expert_ids = jnp.arange(owners, dtype=jnp.int32)
    spread_down = owner_exchange(down_local.reshape(1, owners, width // owners, local_rows))
    spread_proj = owner_exchange(updated.reshape(2, owners, local_rows // owners, width))
    inverse = jnp.sum(
        jnp.where(plan[None, :] == expert_ids[:, None], expert_ids[None, :], 0), axis=1
    )

    def reordered(blocks):
        return jnp.concatenate(
            [lax.dynamic_slice_in_dim(blocks, inverse[e], 1, axis=1) for e in range(owners)], axis=1
        )

    moved_down = owner_exchange(reordered(spread_down))
    moved_proj = owner_exchange(reordered(spread_proj))
    return moved_proj.reshape(2, local_rows, width), moved_down.reshape(width, local_rows)


def generic_body(
    tokens, routes, gates, plan, proj_weight, proj_grad, first_moment, second_moment, down_weight
):
    owners = lax.axis_size("expert")
    local_rows = proj_weight.shape[2]
    group_tokens = tokens.shape[1]
    route_count = routes.shape[2]
    capacity = min(group_tokens, 3 * group_tokens * route_count // (2 * owners))
    down_local = down_weight[0]
    expert_ids = jnp.arange(owners, dtype=jnp.int32)
    target_match = routes[0][:, :, None] == expert_ids[None, None, :]
    routed = jnp.sum(target_match.astype(jnp.int32), axis=1)
    weighting = jnp.sum(jnp.where(target_match, gates[0][:, :, None], 0.0), axis=1)
    token_ids = jnp.arange(group_tokens, dtype=jnp.int32)
    before = (token_ids[None, :] < token_ids[:, None]).astype(jnp.bfloat16)
    ranks = jnp.dot(
        before, routed.astype(jnp.bfloat16), preferred_element_type=jnp.float32
    ).astype(jnp.int32)
    slot_ids = jnp.arange(capacity, dtype=jnp.int32)
    select = jnp.logical_and(
        ranks.T[:, None, :] == slot_ids[None, :, None], routed.T[:, None, :] > 0
    )
    dispatch_buf = jnp.einsum(
        "ost,td->osd", select.astype(jnp.bfloat16), tokens[0], preferred_element_type=jnp.float32
    ).astype(jnp.bfloat16)
    arrived = owner_exchange(dispatch_buf[None])
    slots = arrived.reshape(owners * capacity, local_rows)
    updated = adam_update(proj_weight[0], proj_grad[0], first_moment[0], second_moment[0])
    new_proj, new_down = two_phase_migration(plan, updated, down_local)
    expert_out = finish_rows(dp_blocks(partial_products(slots, updated)), down_local)
    returned = owner_exchange(expert_out.reshape(1, owners, capacity, local_rows))
    combine = select.astype(jnp.float32) * weighting.T[:, None, :]
    mixed = jnp.einsum(
        "ost,osd->td", combine, returned[0].astype(jnp.float32), precision=lax.Precision.HIGHEST
    )
    return (mixed.astype(jnp.bfloat16)[None], new_proj[None], new_down[None])


def foldable(local_rows, width):
    extra = local_rows - width
    return (
        extra > 0
        and width % extra == 0
        and (width // 2) % (width // extra) == 0
        and local_rows % adam_rows == 0
        and ((width // 2) * local_rows // width) % chunk_rows == 0
    )


def lane_slots(sources, targets, lanes, upward):
    count = len(sources)
    order = range(count) if upward else range(count - 1, -1, -1)
    lane_of, moves, done = {}, {}, []
    for e in order:
        moves[e] = targets[e] > sources[e] if upward else targets[e] < sources[e]
        lane = jnp.int32(0)
        found = jnp.bool_(False)
        for k in range(lanes):
            taken = jnp.bool_(False)
            for p in done:
                if upward:
                    open_still = targets[p] > sources[e]
                else:
                    open_still = targets[p] < sources[e]
                taken = taken | (moves[p] & open_still & (lane_of[p] == k))
            lane = jnp.where(jnp.logical_not(found) & jnp.logical_not(taken), k, lane)
            found = found | jnp.logical_not(taken)
        lane_of[e] = lane
        done.append(e)
    return lane_of, moves


def step_kernel(
    lanes,
    plan,
    routes,
    gates,
    tokens,
    weight_hbm,
    grad_hbm,
    first_hbm,
    second_hbm,
    down_hbm,
    out_tokens,
    final,
    own,
    cross,
    stage_up,
    stage_down,
    got_up,
    got_down,
    stage_final,
    weight_buf,
    grad_buf,
    first_buf,
    second_buf,
    down_buf,
    slots,
    partial_out,
    partial_in,
    hidden,
    weighted,
    pair_out,
    pair_in,
    sums,
    returned,
    fold_sem,
    down_sem,
    adam_sem,
    cross_send,
    cross_recv,
    up_send,
    up_recv,
    down_send,
    down_recv,
    final_send,
    final_recv,
    token_send,
    token_recv,
    partial_send,
    partial_recv,
    hidden_send,
    hidden_recv,
    pair_send,
    pair_recv,
    return_send,
    return_recv,
):
    owners = lax.axis_size("expert")
    parts = lax.axis_size("dp")
    levels = owners // 2
    local_rows, width = weight_hbm.shape[2:]
    half_width = width // 2
    extra = local_rows - width
    strips = width // extra
    tall = half_width // strips
    folded = half_width * local_rows // width
    total = folded + local_rows
    chunks, down_chunks = total // chunk_rows, folded // chunk_rows
    blocks = local_rows // adam_rows
    group = tokens.shape[1]
    per_part = owners * group // parts
    spare_lanes = slots.shape[2] - local_rows
    me, my_part = lax.axis_index("expert"), lax.axis_index("dp")
    level, line = me // 2, me % 2
    partner = 2 * level + 1 - line

    def rows_of(c):
        return pl.ds(pl.multiple_of(c * chunk_rows, chunk_rows), chunk_rows)

    def peer(r):
        return lax.rem(me + r, owners)

    def part_peer(r):
        return lax.rem(my_part + r, parts)

    def fold_copies():
        made = []
        for h in (0, 1):
            made.append(
                pltpu.make_async_copy(
                    down_hbm.at[0, pl.ds(h * half_width, half_width), pl.ds(0, width)],
                    own.at[h, pl.ds(0, half_width), :],
                    fold_sem,
                )
            )
            for i in range(strips):
                made.append(
                    pltpu.make_async_copy(
                        down_hbm.at[0, pl.ds(h * half_width + i * tall, tall), pl.ds(width, extra)],
                        own.at[h, pl.ds(half_width, tall), pl.ds(i * extra, extra)],
                        fold_sem,
                    )
                )
        return made

    def adam_copies(block):
        slot = lax.rem(block, adam_buffers)
        rows = pl.ds(pl.multiple_of(block * adam_rows, adam_rows), adam_rows)
        pairs = (
            (weight_hbm, weight_buf),
            (grad_hbm, grad_buf),
            (first_hbm, first_buf),
            (second_hbm, second_buf),
        )
        return [
            pltpu.make_async_copy(
                source.at[0, :, rows, :], target.at[slot], adam_sem.at[n, slot]
            )
            for n, (source, target) in enumerate(pairs)
        ]

    def cross_copy(c):
        return pltpu.make_async_remote_copy(
            src_ref=own.at[1 - line, rows_of(c), :],
            dst_ref=cross.at[rows_of(c), :],
            send_sem=cross_send,
            recv_sem=cross_recv.at[c],
            device_id={"expert": partner},
        )

    def up_copy(c, target):
        return pltpu.make_async_remote_copy(
            src_ref=stage_up.at[c],
            dst_ref=got_up.at[c],
            send_sem=up_send,
            recv_sem=up_recv.at[c],
            device_id={"expert": target},
        )

    def down_copy(c, target):
        return pltpu.make_async_remote_copy(
            src_ref=stage_down.at[c],
            dst_ref=got_down.at[c],
            send_sem=down_send,
            recv_sem=down_recv.at[c],
            device_id={"expert": target},
        )

    def final_copy(c, h):
        return pltpu.make_async_remote_copy(
            src_ref=stage_final.at[rows_of(c), :],
            dst_ref=final.at[h, rows_of(c), :],
            send_sem=final_send,
            recv_sem=final_recv.at[c],
            device_id={"expert": partner},
        )

    def token_swap(slot):
        return pltpu.make_async_remote_copy(
            src_ref=slots.at[slot],
            dst_ref=slots.at[slot],
            send_sem=token_send.at[0],
            recv_sem=token_recv.at[0],
            device_id={"expert": partner},
        )

    def token_copy(hop, at_level, target, first):
        pair = slots.at[pl.ds(2 * at_level, 2)]
        return pltpu.make_async_remote_copy(
            src_ref=pair,
            dst_ref=pair,
            send_sem=token_send.at[first + hop],
            recv_sem=token_recv.at[first + hop + 1],
            device_id={"expert": target},
        )

    def partial_copy(r, slot):
        return pltpu.make_async_remote_copy(
            src_ref=partial_out.at[part_peer(r)],
            dst_ref=partial_in.at[slot],
            send_sem=partial_send.at[r],
            recv_sem=partial_recv.at[r],
            device_id={"dp": part_peer(r)},
        )

    def hidden_copy(r, slot):
        return pltpu.make_async_remote_copy(
            src_ref=hidden.at[slot],
            dst_ref=hidden.at[slot],
            send_sem=hidden_send.at[r],
            recv_sem=hidden_recv.at[r],
            device_id={"dp": part_peer(r)},
        )

    def pair_copy():
        return pltpu.make_async_remote_copy(
            src_ref=pair_out,
            dst_ref=pair_in,
            send_sem=pair_send,
            recv_sem=pair_recv,
            device_id={"expert": partner},
        )

    def return_copy(d, slot):
        to_level = lax.rem(level + d, levels)
        return pltpu.make_async_remote_copy(
            src_ref=sums.at[to_level],
            dst_ref=returned.at[slot],
            send_sem=return_send.at[d],
            recv_sem=return_recv.at[d],
            device_id={"expert": 2 * to_level + line},
        )

    lanes_of = lax.broadcasted_iota(jnp.int32, (group, spare_lanes), 1)

    def gate_lanes():
        square = (group, group)
        same = lax.broadcasted_iota(jnp.int32, square, 0) == lax.broadcasted_iota(
            jnp.int32, square, 1
        )
        placed = jnp.zeros((group, spare_lanes), jnp.float32)
        for e in range(owners):
            row = jnp.sum(jnp.where(routes[0] == e, gates[0], 0.0), axis=0, keepdims=True)
            rest = jnp.sum(jnp.where(same, row, 0.0), axis=1, keepdims=True)
            for part in range(3):
                piece = rest.astype(jnp.bfloat16).astype(jnp.float32)
                placed = jnp.where(lanes_of == part * owners + e, piece, placed)
                rest = rest - piece
        return placed.astype(jnp.bfloat16)

    for copy in fold_copies():
        copy.start()
    for block in range(adam_buffers):
        for copy in adam_copies(jnp.int32(block)):
            copy.start()
    down_load = pltpu.make_async_copy(down_hbm.at[0], down_buf, down_sem)
    down_load.start()
    slots[me, :, pl.ds(0, local_rows)] = tokens[0]
    slots[me, :, pl.ds(local_rows, spare_lanes)] = gate_lanes()

    barrier = pltpu.get_barrier_semaphore()
    for r in range(1, owners):
        pl.semaphore_signal(barrier, inc=1, device_id={"expert": peer(r)})
    for r in range(1, parts):
        pl.semaphore_signal(barrier, inc=1, device_id={"dp": part_peer(r)})
    pl.semaphore_wait(barrier, owners + parts - 2)

    pltpu.make_async_copy(
        own.at[:, pl.ds(0, folded), :], own.at[:, pl.ds(0, folded), :], fold_sem
    ).wait()
    for c in range(lead):
        cross_copy(c).start()
        if c == 0:
            token_swap(me).start()

    sources = [e // 2 for e in range(owners)]
    targets = [plan[e] // 2 for e in range(owners)]
    up_lane, goes_up = lane_slots(sources, targets, lanes, True)
    down_lane, goes_down = lane_slots(sources, targets, lanes, False)

    def at_me(values):
        mine, other = jnp.int32(-1), jnp.int32(-1)
        for e in range(owners):
            mine = jnp.where(me == e, values[e], mine)
            other = jnp.where(partner == e, values[e], other)
        return mine, other

    up_mine, up_other = at_me([jnp.where(goes_up[e], up_lane[e], -1) for e in range(owners)])
    down_mine, down_other = at_me(
        [jnp.where(goes_down[e], down_lane[e], -1) for e in range(owners)]
    )
    origin_mine, origin_other = jnp.int32(0), jnp.int32(0)
    for e in range(owners):
        origin = jnp.where(
            goes_up[e] & (level != sources[e]),
            2 + up_lane[e],
            jnp.where(
                goes_down[e] & (level != sources[e]),
                2 + lanes + down_lane[e],
                jnp.where(me == e, 0, 1),
            ),
        )
        origin_mine = jnp.where(plan[e] == me, origin, origin_mine)
        origin_other = jnp.where(plan[e] == partner, origin, origin_other)

    def forward(c, got, stage, lane_mine, lane_other):
        mine = own[line, rows_of(c), :]
        other = cross[rows_of(c), :]
        for k in range(lanes):
            value = jnp.where(lane_mine == k, mine, got[c, k])
            stage[c, k] = jnp.where(lane_other == k, other, value)

    def adam_block(i):
        for copy in adam_copies(i):
            copy.wait()
        slot = lax.rem(i, adam_buffers)
        strips_of = adam_rows // 16

        def strip(j, unused):
            h = j // strips_of
            at = pl.multiple_of((j % strips_of) * 16, 16)
            rows = pl.ds(at, 16)
            grad = grad_buf[slot, h, rows, :].astype(jnp.float32)
            first = beta_first * first_buf[slot, h, rows, :] + (1.0 - beta_first) * grad
            second = beta_second * second_buf[slot, h, rows, :] + (1.0 - beta_second) * grad * grad
            scaled = first * (learning_rate / bias_first)
            denominator = jnp.sqrt(second * (1.0 / bias_second)) + adam_epsilon
            value = weight_buf[slot, h, rows, :].astype(jnp.float32) - scaled / denominator
            start = pl.multiple_of(folded + i * adam_rows + at, 16)
            own[h, pl.ds(start, 16), :] = value.astype(jnp.bfloat16)
            return unused

        lax.fori_loop(0, 2 * strips_of, strip, 0)

        @pl.when(i + adam_buffers < blocks)
        def _():
            for copy in adam_copies(i + adam_buffers):
                copy.start()

    def pass_tokens(hop):
        @pl.when(hop == 0)
        def _():
            token_swap(partner).wait_recv()

        for first, from_level, edge, target in (
            (1, level - hop, levels - 1, me + 2),
            (1 + levels, level + hop, 0, me - 2),
        ):

            @pl.when((from_level >= 0) & (from_level < levels))
            def _():
                @pl.when(hop > 0)
                def _():
                    token_copy(hop - 1, from_level, me, first).wait_recv()

                @pl.when(level != edge)
                def _():
                    token_copy(hop, from_level, target, first).start()

    def send_partials():
        gathered = slots[:, :, pl.ds(0, local_rows)].reshape(owners * group, local_rows)
        for h in (0, 1):
            product = jnp.dot(
                gathered, own[h, pl.ds(folded, local_rows), :], preferred_element_type=jnp.float32
            )
            partial_out[:, :, pl.ds(h * width, width)] = product.astype(jnp.bfloat16).reshape(
                parts, per_part, width
            )
        for r in range(1, parts):
            partial_copy(r, my_part).start()
        partial_in[my_part] = partial_out[my_part]

    def send_hidden():
        for r in range(1, parts):
            partial_copy(r, lax.rem(my_part + parts - r, parts)).wait_recv()
        summed = partial_in[0].astype(jnp.float32)
        for p in range(1, parts):
            summed = summed + partial_in[p].astype(jnp.float32)
        gate, up = summed[:, :width], summed[:, width:]
        hidden[my_part] = (gate / (1.0 + jnp.exp(-gate)) * up).astype(jnp.bfloat16)
        for r in range(1, parts):
            hidden_copy(r, my_part).start()

    def make_results():
        for r in range(1, parts):
            hidden_copy(r, lax.rem(my_part + parts - r, parts)).wait_recv()
        down_load.wait()
        product = jnp.dot(
            hidden[...].reshape(owners * group, width),
            down_buf[...],
            preferred_element_type=jnp.float32,
        )
        results = product.astype(jnp.bfloat16).astype(jnp.float32)
        results = results.reshape(owners, group, local_rows)
        for e in range(owners):
            pieces = slots[e, :, pl.ds(local_rows, spare_lanes)].astype(jnp.float32)
            gate = jnp.sum(
                jnp.where(lax.rem(lanes_of, owners) == me, pieces, 0.0), axis=1, keepdims=True
            )
            weighted[e] = gate * results[e]
        for l in range(levels):
            pair_out[l] = weighted[2 * l + 1 - line].astype(jnp.bfloat16)
        pair_copy().start()

    def send_results():
        pair_copy().wait_recv()
        for l in range(levels):
            total_of = weighted[2 * l + line] + pair_in[l].astype(jnp.float32)
            sums[l] = total_of.astype(jnp.bfloat16)
        for d in range(1, levels):
            return_copy(d, level).start()

    def mix_results():
        mixed = weighted[me] + pair_in[level].astype(jnp.float32)
        for d in range(1, levels):
            source = lax.rem(level + levels - d, levels)
            return_copy(d, source).wait_recv()
            mixed = mixed + returned[source].astype(jnp.float32)
        out_tokens[0] = mixed.astype(jnp.bfloat16)

    skew = skews[lanes]
    reach = (levels - 1) * skew

    def step(i, unused):
        @pl.when(i + lead < chunks)
        def _():
            cross_copy(i + lead).start()

        cross_at = i - jnp.minimum(level, levels - 1 - level) * skew

        @pl.when((cross_at >= 0) & (cross_at < chunks))
        def _():
            cross_copy(cross_at).wait_recv()

        up_at = i - level * skew

        @pl.when((up_at >= 0) & (up_at < chunks))
        def _():
            @pl.when(level > 0)
            def _():
                up_copy(up_at, me).wait_recv()

            @pl.when(level < levels - 1)
            def _():
                forward(up_at, got_up, stage_up, up_mine, up_other)
                up_copy(up_at, me + 2).start()

        down_at = i - (levels - 1 - level) * skew

        @pl.when((down_at >= 0) & (down_at < chunks))
        def _():
            @pl.when(level < levels - 1)
            def _():
                down_copy(down_at, me).wait_recv()

            @pl.when(level > 0)
            def _():
                forward(down_at, got_down, stage_down, down_mine, down_other)
                down_copy(down_at, me - 2).start()

        at = i - reach

        @pl.when((at >= 0) & (at < chunks))
        def _():
            mine = own[line, rows_of(at), :]
            other = cross[rows_of(at), :]
            keep = jnp.where(origin_mine == 0, mine, other)
            give = jnp.where(origin_other == 0, mine, other)
            for k in range(lanes):
                value = got_up[at, k]
                keep = jnp.where(origin_mine == 2 + k, value, keep)
                give = jnp.where(origin_other == 2 + k, value, give)
                value = got_down[at, k]
                keep = jnp.where(origin_mine == 2 + lanes + k, value, keep)
                give = jnp.where(origin_other == 2 + lanes + k, value, give)
            stage_final[rows_of(at), :] = give
            final_copy(at, line).start()
            final[line, rows_of(at), :] = keep

        landed = i - reach - lag

        @pl.when((landed >= 0) & (landed < chunks))
        def _():
            final_copy(landed, 1 - line).wait_recv()

        @pl.when(i < blocks)
        def _():
            adam_block(i)

        since = i - pass_from

        @pl.when((since >= 0) & (since < levels * pass_every) & (since % pass_every == 0))
        def _():
            pass_tokens(since // pass_every)

        work = (send_partials, send_hidden, make_results, send_results)
        for when, job in zip(token_steps + (chunks + skew + return_step,), work):
            pl.when(i == when)(job)
        return unused

    lax.fori_loop(0, chunks + reach + lag, step, 0)
    mix_results()

    token_swap(me).wait_send()
    for hop in range(levels - 1):

        @pl.when((level - hop >= 0) & (level < levels - 1))
        def _():
            token_copy(hop, level - hop, me, 1).wait_send()

        @pl.when((level + hop < levels) & (level > 0))
        def _():
            token_copy(hop, level + hop, me, 1 + levels).wait_send()

    pair_copy().wait_send()
    for d in range(1, levels):
        return_copy(d, level).wait_send()
    for r in range(1, parts):
        partial_copy(r, my_part).wait_send()
        hidden_copy(r, my_part).wait_send()

    def whole_wait(buffer, sem):
        pltpu.make_async_remote_copy(
            src_ref=buffer, dst_ref=buffer, send_sem=sem, recv_sem=sem, device_id={"expert": partner}
        ).wait_send()

    whole_wait(cross, cross_send)
    whole_wait(stage_final, final_send)

    @pl.when(level < levels - 1)
    def _():
        whole_wait(stage_up, up_send)

    @pl.when(level > 0)
    def _():
        whole_wait(stage_down, down_send)


def write_kernel(tokens, final, out_tokens, new_proj, new_down, sem):
    local_rows, width = new_proj.shape[2:]
    half_width = width // 2
    extra = local_rows - width
    tall = half_width // (width // extra)
    folded = final.shape[1] - local_rows
    copies = [(tokens, out_tokens)]
    for h in (0, 1):
        copies.append((final.at[h, pl.ds(folded, local_rows), :], new_proj.at[0, h]))
        rows = pl.ds(h * half_width, half_width)
        copies.append((final.at[h, pl.ds(0, half_width), :], new_down.at[0, rows, pl.ds(0, width)]))
        for i in range(width // extra):
            rows = pl.ds(h * half_width + i * tall, tall)
            copies.append(
                (
                    final.at[h, pl.ds(half_width, tall), pl.ds(i * extra, extra)],
                    new_down.at[0, rows, pl.ds(width, extra)],
                )
            )
    made = [pltpu.make_async_copy(a, b, sem.at[n]) for n, (a, b) in enumerate(copies)]
    for copy in made:
        copy.start()
    for copy in made:
        copy.wait()


def write_call(tokens, final, weights, down):
    copies = 3 + 2 * (1 + down.shape[1] // (down.shape[2] - down.shape[1]))
    hbm = pl.BlockSpec(memory_space=pl.ANY)
    return pl.pallas_call(
        write_kernel,
        out_shape=[jax.ShapeDtypeStruct(a.shape, a.dtype) for a in (tokens, weights, down)],
        in_specs=[hbm, hbm],
        out_specs=[hbm, hbm, hbm],
        scratch_shapes=[pltpu.SemaphoreType.DMA((copies,))],
        compiler_params=pltpu.CompilerParams(vmem_limit_bytes=2**20),
        cost_estimate=pl.CostEstimate(
            flops=0, bytes_accessed=4 * final.size + 4 * tokens.size, transcendentals=0
        ),
        name="write_results",
    )(tokens, final)


def step_call(lanes, tokens, routes, gates, plan, weights, grads, first, second, down):
    owners, parts = lax.axis_size("expert"), lax.axis_size("dp")
    local_rows, width = weights.shape[2:]
    group = tokens.shape[1]
    folded = (width // 2) * local_rows // width
    total = folded + local_rows
    chunks = total // chunk_rows
    per_part = owners * group // parts
    bf16, f32 = jnp.bfloat16, jnp.float32
    lane_buffer = pltpu.VMEM((chunks, lanes, chunk_rows, width), bf16)
    adam_shape = (adam_buffers, 2, adam_rows, width)
    dma = pltpu.SemaphoreType.DMA
    vmem = pl.BlockSpec(memory_space=pltpu.VMEM)
    hbm = pl.BlockSpec(memory_space=pl.ANY)
    moved = 2 * total * width * 2
    return pl.pallas_call(
        functools.partial(step_kernel, lanes),
        out_shape=(
            jax.ShapeDtypeStruct(tokens.shape, bf16),
            pltpu.VMEM((2, total, width), bf16),
        ),
        in_specs=[pl.BlockSpec(memory_space=pltpu.SMEM), vmem, vmem, vmem] + [hbm] * 5,
        out_specs=(vmem, vmem),
        scratch_shapes=[
            pltpu.VMEM((2, total, width), bf16),
            pltpu.VMEM((total, width), bf16),
            lane_buffer,
            lane_buffer,
            lane_buffer,
            lane_buffer,
            pltpu.VMEM((total, width), bf16),
            pltpu.VMEM(adam_shape, bf16),
            pltpu.VMEM(adam_shape, bf16),
            pltpu.VMEM(adam_shape, f32),
            pltpu.VMEM(adam_shape, f32),
            pltpu.VMEM((width, local_rows), bf16),
            pltpu.VMEM((owners, group, local_rows + 128), bf16),
            pltpu.VMEM((parts, per_part, 2 * width), bf16),
            pltpu.VMEM((parts, per_part, 2 * width), bf16),
            pltpu.VMEM((parts, per_part, width), bf16),
            pltpu.VMEM((owners, group, local_rows), f32),
            pltpu.VMEM((owners // 2, group, local_rows), bf16),
            pltpu.VMEM((owners // 2, group, local_rows), bf16),
            pltpu.VMEM((owners // 2, group, local_rows), bf16),
            pltpu.VMEM((owners // 2, group, local_rows), bf16),
            dma,
            dma,
            dma((4, adam_buffers)),
            dma,
            dma((chunks,)),
            dma,
            dma((chunks,)),
            dma,
            dma((chunks,)),
            dma,
            dma((chunks,)),
            dma((owners + 1,)),
            dma((owners + 1,)),
            dma((parts,)),
            dma((parts,)),
            dma((parts,)),
            dma((parts,)),
            dma,
            dma,
            dma((owners,)),
            dma((owners,)),
        ],
        compiler_params=pltpu.CompilerParams(
            collective_id=lanes, has_side_effects=True, vmem_limit_bytes=vmem_limit[lanes] * 2**20
        ),
        cost_estimate=pl.CostEstimate(
            flops=6 * owners * group * local_rows * width,
            bytes_accessed=6 * moved,
            transcendentals=2 * local_rows * width,
        ),
        name=f"adam_migrate_route_{lanes}",
    )(plan, jnp.swapaxes(routes, 1, 2), jnp.swapaxes(gates, 1, 2), tokens, weights, grads, first, second, down)


def body(
    tokens, routes, gates, plan, proj_weight, proj_grad, first_moment, second_moment, down_weight
):
    args = (tokens, routes, gates, plan, proj_weight, proj_grad, first_moment, second_moment, down_weight)
    owners = lax.axis_size("expert")
    levels = owners // 2
    if levels > max_levels or owners != routes.shape[2] or not foldable(*proj_weight.shape[2:]):
        return generic_body(*args)
    fewest = min(2, levels)
    choices = range(fewest, levels + 1)
    expert_ids = jnp.arange(owners, dtype=jnp.int32)
    crossing = [
        jnp.sum(((expert_ids < 2 * cut) & (plan >= 2 * cut)).astype(jnp.int32))
        for cut in range(2, levels - 1)
    ]
    widest = functools.reduce(jnp.maximum, crossing, jnp.int32(fewest))

    def step_with(lanes):
        return lambda *args: write_call(*step_call(lanes, *args), proj_weight, down_weight)

    return lax.switch(widest - fewest, [step_with(lanes) for lanes in choices], *args)


def solution(mesh):
    in_specs = (
        P("expert", None, "dp"),
        P("expert", None, None),
        P("expert", None, None),
        P(),
        P("expert", None, "dp", None),
        P("expert", None, "dp", None),
        P("expert", None, "dp", None),
        P("expert", None, "dp", None),
        P("expert", None, "dp"),
    )
    out_specs = (P("expert", None, "dp"), P("expert", None, "dp", None), P("expert", None, "dp"))
    return jax.shard_map(body, mesh=mesh, in_specs=in_specs, out_specs=out_specs, check_vma=False)
```

```python
import functools

import jax
import jax.numpy as jnp
from jax import lax
from jax.experimental import pallas as pl
from jax.experimental.pallas import tpu as pltpu
from jax.sharding import PartitionSpec as P

learning_rate = 0.01
beta_first = 0.9
beta_second = 0.999
adam_epsilon = 1e-08
bias_first = 1.0 - 0.9**10
bias_second = 1.0 - 0.999**10

chunk_rows = 16
adam_rows = 64
adam_buffers = 4
skews = {1: 4, 2: 4, 3: 3, 4: 3}
lead = 14
lag = 5
pass_from = 0
pass_every = 3
token_steps = (20, 30, 40)
return_step = 3
max_levels = 4
vmem_limit = {2: 38, 3: 48, 4: 54}


def adam_update(weights, grads, first_moment, second_moment):
    grad_float = grads.astype(jnp.float32)
    first_new = beta_first * first_moment + (1.0 - beta_first) * grad_float
    second_new = beta_second * second_moment + (1.0 - beta_second) * grad_float * grad_float
    adam_step = first_new / bias_first / (jnp.sqrt(second_new / bias_second) + adam_epsilon)
    return (weights.astype(jnp.float32) - learning_rate * adam_step).astype(jnp.bfloat16)


def partial_products(slots, updated):
    joined = jnp.concatenate([updated[0], updated[1]], axis=1)
    return jnp.dot(slots, joined, preferred_element_type=jnp.float32).astype(jnp.bfloat16)


def dp_blocks(partials):
    parts = lax.axis_size("dp")
    return lax.all_to_all(
        partials.reshape(1, parts, -1, partials.shape[1]),
        "dp",
        split_axis=1,
        concat_axis=1,
        tiled=True,
    )


def finish_rows(blocks, down_local):
    width = down_local.shape[0]
    summed = jnp.sum(blocks[0].astype(jnp.float32), axis=0)
    hidden = (jax.nn.silu(summed[:, :width]) * summed[:, width:]).astype(jnp.bfloat16)
    result = jnp.dot(
        lax.all_gather(hidden, "dp", axis=0, tiled=True),
        down_local,
        preferred_element_type=jnp.float32,
    )
    return result.astype(jnp.bfloat16)


def owner_exchange(pieces):
    return lax.all_to_all(pieces, "expert", split_axis=1, concat_axis=1, tiled=True)


def two_phase_migration(plan, updated, down_local):
    owners = lax.axis_size("expert")
    local_rows, width = updated.shape[1:]
    expert_ids = jnp.arange(owners, dtype=jnp.int32)
    spread_down = owner_exchange(down_local.reshape(1, owners, width // owners, local_rows))
    spread_proj = owner_exchange(updated.reshape(2, owners, local_rows // owners, width))
    inverse = jnp.sum(
        jnp.where(plan[None, :] == expert_ids[:, None], expert_ids[None, :], 0), axis=1
    )

    def reordered(blocks):
        return jnp.concatenate(
            [lax.dynamic_slice_in_dim(blocks, inverse[e], 1, axis=1) for e in range(owners)], axis=1
        )

    moved_down = owner_exchange(reordered(spread_down))
    moved_proj = owner_exchange(reordered(spread_proj))
    return moved_proj.reshape(2, local_rows, width), moved_down.reshape(width, local_rows)


def generic_body(
    tokens, routes, gates, plan, proj_weight, proj_grad, first_moment, second_moment, down_weight
):
    owners = lax.axis_size("expert")
    local_rows = proj_weight.shape[2]
    group_tokens = tokens.shape[1]
    route_count = routes.shape[2]
    capacity = min(group_tokens, 3 * group_tokens * route_count // (2 * owners))
    down_local = down_weight[0]
    expert_ids = jnp.arange(owners, dtype=jnp.int32)
    target_match = routes[0][:, :, None] == expert_ids[None, None, :]
    routed = jnp.sum(target_match.astype(jnp.int32), axis=1)
    weighting = jnp.sum(jnp.where(target_match, gates[0][:, :, None], 0.0), axis=1)
    token_ids = jnp.arange(group_tokens, dtype=jnp.int32)
    before = (token_ids[None, :] < token_ids[:, None]).astype(jnp.bfloat16)
    ranks = jnp.dot(
        before, routed.astype(jnp.bfloat16), preferred_element_type=jnp.float32
    ).astype(jnp.int32)
    slot_ids = jnp.arange(capacity, dtype=jnp.int32)
    select = jnp.logical_and(
        ranks.T[:, None, :] == slot_ids[None, :, None], routed.T[:, None, :] > 0
    )
    dispatch_buf = jnp.einsum(
        "ost,td->osd", select.astype(jnp.bfloat16), tokens[0], preferred_element_type=jnp.float32
    ).astype(jnp.bfloat16)
    arrived = owner_exchange(dispatch_buf[None])
    slots = arrived.reshape(owners * capacity, local_rows)
    updated = adam_update(proj_weight[0], proj_grad[0], first_moment[0], second_moment[0])
    new_proj, new_down = two_phase_migration(plan, updated, down_local)
    expert_out = finish_rows(dp_blocks(partial_products(slots, updated)), down_local)
    returned = owner_exchange(expert_out.reshape(1, owners, capacity, local_rows))
    combine = select.astype(jnp.float32) * weighting.T[:, None, :]
    mixed = jnp.einsum(
        "ost,osd->td", combine, returned[0].astype(jnp.float32), precision=lax.Precision.HIGHEST
    )
    return (mixed.astype(jnp.bfloat16)[None], new_proj[None], new_down[None])


def foldable(local_rows, width):
    extra = local_rows - width
    return (
        extra > 0
        and width % extra == 0
        and (width // 2) % (width // extra) == 0
        and local_rows % adam_rows == 0
        and ((width // 2) * local_rows // width) % chunk_rows == 0
    )


def lane_slots(sources, targets, lanes, upward):
    count = len(sources)
    order = range(count) if upward else range(count - 1, -1, -1)
    lane_of, moves, done = {}, {}, []
    for e in order:
        moves[e] = targets[e] > sources[e] if upward else targets[e] < sources[e]
        lane = jnp.int32(0)
        found = jnp.bool_(False)
        for k in range(lanes):
            taken = jnp.bool_(False)
            for p in done:
                if upward:
                    open_still = targets[p] > sources[e]
                else:
                    open_still = targets[p] < sources[e]
                taken = taken | (moves[p] & open_still & (lane_of[p] == k))
            lane = jnp.where(jnp.logical_not(found) & jnp.logical_not(taken), k, lane)
            found = found | jnp.logical_not(taken)
        lane_of[e] = lane
        done.append(e)
    return lane_of, moves


def step_kernel(
    lanes,
    plan,
    routes,
    gates,
    tokens,
    weight_hbm,
    grad_hbm,
    first_hbm,
    second_hbm,
    down_hbm,
    out_tokens,
    final,
    own,
    cross,
    stage_up,
    stage_down,
    got_up,
    got_down,
    stage_final,
    weight_buf,
    grad_buf,
    first_buf,
    second_buf,
    down_buf,
    slots,
    partial_out,
    partial_in,
    hidden,
    weighted,
    pair_out,
    pair_in,
    sums,
    returned,
    fold_sem,
    down_sem,
    adam_sem,
    cross_send,
    cross_recv,
    up_send,
    up_recv,
    down_send,
    down_recv,
    final_send,
    final_recv,
    token_send,
    token_recv,
    partial_send,
    partial_recv,
    hidden_send,
    hidden_recv,
    pair_send,
    pair_recv,
    return_send,
    return_recv,
):
    owners = lax.axis_size("expert")
    parts = lax.axis_size("dp")
    levels = owners // 2
    local_rows, width = weight_hbm.shape[2:]
    half_width = width // 2
    extra = local_rows - width
    strips = width // extra
    tall = half_width // strips
    folded = half_width * local_rows // width
    total = folded + local_rows
    chunks, down_chunks = total // chunk_rows, folded // chunk_rows
    blocks = local_rows // adam_rows
    group = tokens.shape[1]
    per_part = owners * group // parts
    spare_lanes = slots.shape[2] - local_rows
    me, my_part = lax.axis_index("expert"), lax.axis_index("dp")
    level, line = me // 2, me % 2
    partner = 2 * level + 1 - line

    def rows_of(c):
        return pl.ds(pl.multiple_of(c * chunk_rows, chunk_rows), chunk_rows)

    def peer(r):
        return lax.rem(me + r, owners)

    def part_peer(r):
        return lax.rem(my_part + r, parts)

    def fold_copies():
        made = []
        for h in (0, 1):
            made.append(
                pltpu.make_async_copy(
                    down_hbm.at[0, pl.ds(h * half_width, half_width), pl.ds(0, width)],
                    own.at[h, pl.ds(0, half_width), :],
                    fold_sem,
                )
            )
            for i in range(strips):
                made.append(
                    pltpu.make_async_copy(
                        down_hbm.at[0, pl.ds(h * half_width + i * tall, tall), pl.ds(width, extra)],
                        own.at[h, pl.ds(half_width, tall), pl.ds(i * extra, extra)],
                        fold_sem,
                    )
                )
        return made

    def adam_copies(block):
        slot = lax.rem(block, adam_buffers)
        rows = pl.ds(pl.multiple_of(block * adam_rows, adam_rows), adam_rows)
        pairs = (
            (weight_hbm, weight_buf),
            (grad_hbm, grad_buf),
            (first_hbm, first_buf),
            (second_hbm, second_buf),
        )
        return [
            pltpu.make_async_copy(
                source.at[0, :, rows, :], target.at[slot], adam_sem.at[n, slot]
            )
            for n, (source, target) in enumerate(pairs)
        ]

    def cross_copy(c):
        return pltpu.make_async_remote_copy(
            src_ref=own.at[1 - line, rows_of(c), :],
            dst_ref=cross.at[rows_of(c), :],
            send_sem=cross_send,
            recv_sem=cross_recv.at[c],
            device_id={"expert": partner},
        )

    def up_copy(c, target):
        return pltpu.make_async_remote_copy(
            src_ref=stage_up.at[c],
            dst_ref=got_up.at[c],
            send_sem=up_send,
            recv_sem=up_recv.at[c],
            device_id={"expert": target},
        )

    def down_copy(c, target):
        return pltpu.make_async_remote_copy(
            src_ref=stage_down.at[c],
            dst_ref=got_down.at[c],
            send_sem=down_send,
            recv_sem=down_recv.at[c],
            device_id={"expert": target},
        )

    def final_copy(c, h):
        return pltpu.make_async_remote_copy(
            src_ref=stage_final.at[rows_of(c), :],
            dst_ref=final.at[h, rows_of(c), :],
            send_sem=final_send,
            recv_sem=final_recv.at[c],
            device_id={"expert": partner},
        )

    def token_swap(slot):
        return pltpu.make_async_remote_copy(
            src_ref=slots.at[slot],
            dst_ref=slots.at[slot],
            send_sem=token_send.at[0],
            recv_sem=token_recv.at[0],
            device_id={"expert": partner},
        )

    def token_copy(hop, at_level, target, first):
        pair = slots.at[pl.ds(2 * at_level, 2)]
        return pltpu.make_async_remote_copy(
            src_ref=pair,
            dst_ref=pair,
            send_sem=token_send.at[first + hop],
            recv_sem=token_recv.at[first + hop + 1],
            device_id={"expert": target},
        )

    def partial_copy(r, slot):
        return pltpu.make_async_remote_copy(
            src_ref=partial_out.at[part_peer(r)],
            dst_ref=partial_in.at[slot],
            send_sem=partial_send.at[r],
            recv_sem=partial_recv.at[r],
            device_id={"dp": part_peer(r)},
        )

    def hidden_copy(r, slot):
        return pltpu.make_async_remote_copy(
            src_ref=hidden.at[slot],
            dst_ref=hidden.at[slot],
            send_sem=hidden_send.at[r],
            recv_sem=hidden_recv.at[r],
            device_id={"dp": part_peer(r)},
        )

    def pair_copy():
        return pltpu.make_async_remote_copy(
            src_ref=pair_out,
            dst_ref=pair_in,
            send_sem=pair_send,
            recv_sem=pair_recv,
            device_id={"expert": partner},
        )

    def return_copy(d, slot):
        to_level = lax.rem(level + d, levels)
        return pltpu.make_async_remote_copy(
            src_ref=sums.at[to_level],
            dst_ref=returned.at[slot],
            send_sem=return_send.at[d],
            recv_sem=return_recv.at[d],
            device_id={"expert": 2 * to_level + line},
        )

    lanes_of = lax.broadcasted_iota(jnp.int32, (group, spare_lanes), 1)

    def gate_lanes():
        square = (group, group)
        same = lax.broadcasted_iota(jnp.int32, square, 0) == lax.broadcasted_iota(
            jnp.int32, square, 1
        )
        placed = jnp.zeros((group, spare_lanes), jnp.float32)
        for e in range(owners):
            row = jnp.sum(jnp.where(routes[0] == e, gates[0], 0.0), axis=0, keepdims=True)
            rest = jnp.sum(jnp.where(same, row, 0.0), axis=1, keepdims=True)
            for part in range(3):
                piece = rest.astype(jnp.bfloat16).astype(jnp.float32)
                placed = jnp.where(lanes_of == part * owners + e, piece, placed)
                rest = rest - piece
        return placed.astype(jnp.bfloat16)

    for copy in fold_copies():
        copy.start()
    for block in range(adam_buffers):
        for copy in adam_copies(jnp.int32(block)):
            copy.start()
    down_load = pltpu.make_async_copy(down_hbm.at[0], down_buf, down_sem)
    down_load.start()
    slots[me, :, pl.ds(0, local_rows)] = tokens[0]
    slots[me, :, pl.ds(local_rows, spare_lanes)] = gate_lanes()

    barrier = pltpu.get_barrier_semaphore()
    for r in range(1, owners):
        pl.semaphore_signal(barrier, inc=1, device_id={"expert": peer(r)})
    for r in range(1, parts):
        pl.semaphore_signal(barrier, inc=1, device_id={"dp": part_peer(r)})
    pl.semaphore_wait(barrier, owners + parts - 2)

    pltpu.make_async_copy(
        own.at[:, pl.ds(0, folded), :], own.at[:, pl.ds(0, folded), :], fold_sem
    ).wait()
    for c in range(lead):
        cross_copy(c).start()
        if c == 0:
            token_swap(me).start()

    sources = [e // 2 for e in range(owners)]
    targets = [plan[e] // 2 for e in range(owners)]
    up_lane, goes_up = lane_slots(sources, targets, lanes, True)
    down_lane, goes_down = lane_slots(sources, targets, lanes, False)

    def at_me(values):
        mine, other = jnp.int32(-1), jnp.int32(-1)
        for e in range(owners):
            mine = jnp.where(me == e, values[e], mine)
            other = jnp.where(partner == e, values[e], other)
        return mine, other

    up_mine, up_other = at_me([jnp.where(goes_up[e], up_lane[e], -1) for e in range(owners)])
    down_mine, down_other = at_me(
        [jnp.where(goes_down[e], down_lane[e], -1) for e in range(owners)]
    )
    origin_mine, origin_other = jnp.int32(0), jnp.int32(0)
    for e in range(owners):
        origin = jnp.where(
            goes_up[e] & (level != sources[e]),
            2 + up_lane[e],
            jnp.where(
                goes_down[e] & (level != sources[e]),
                2 + lanes + down_lane[e],
                jnp.where(me == e, 0, 1),
            ),
        )
        origin_mine = jnp.where(plan[e] == me, origin, origin_mine)
        origin_other = jnp.where(plan[e] == partner, origin, origin_other)

    def forward(c, got, stage, lane_mine, lane_other):
        mine = own[line, rows_of(c), :]
        other = cross[rows_of(c), :]
        for k in range(lanes):
            value = jnp.where(lane_mine == k, mine, got[c, k])
            stage[c, k] = jnp.where(lane_other == k, other, value)

    def adam_block(i):
        for copy in adam_copies(i):
            copy.wait()
        slot = lax.rem(i, adam_buffers)
        strips_of = adam_rows // 16

        def strip(j, unused):
            h = j // strips_of
            at = pl.multiple_of((j % strips_of) * 16, 16)
            rows = pl.ds(at, 16)
            grad = grad_buf[slot, h, rows, :].astype(jnp.float32)
            first = beta_first * first_buf[slot, h, rows, :] + (1.0 - beta_first) * grad
            second = beta_second * second_buf[slot, h, rows, :] + (1.0 - beta_second) * grad * grad
            scaled = first * (learning_rate / bias_first)
            denominator = jnp.sqrt(second * (1.0 / bias_second)) + adam_epsilon
            value = weight_buf[slot, h, rows, :].astype(jnp.float32) - scaled / denominator
            start = pl.multiple_of(folded + i * adam_rows + at, 16)
            own[h, pl.ds(start, 16), :] = value.astype(jnp.bfloat16)
            return unused

        lax.fori_loop(0, 2 * strips_of, strip, 0)

        @pl.when(i + adam_buffers < blocks)
        def _():
            for copy in adam_copies(i + adam_buffers):
                copy.start()

    def pass_tokens(hop):
        @pl.when(hop == 0)
        def _():
            token_swap(partner).wait_recv()

        for first, from_level, edge, target in (
            (1, level - hop, levels - 1, me + 2),
            (1 + levels, level + hop, 0, me - 2),
        ):

            @pl.when((from_level >= 0) & (from_level < levels))
            def _():
                @pl.when(hop > 0)
                def _():
                    token_copy(hop - 1, from_level, me, first).wait_recv()

                @pl.when(level != edge)
                def _():
                    token_copy(hop, from_level, target, first).start()

    def send_partials():
        gathered = slots[:, :, pl.ds(0, local_rows)].reshape(owners * group, local_rows)
        for h in (0, 1):
            product = jnp.dot(
                gathered, own[h, pl.ds(folded, local_rows), :], preferred_element_type=jnp.float32
            )
            partial_out[:, :, pl.ds(h * width, width)] = product.astype(jnp.bfloat16).reshape(
                parts, per_part, width
            )
        for r in range(1, parts):
            partial_copy(r, my_part).start()
        partial_in[my_part] = partial_out[my_part]

    def send_hidden():
        for r in range(1, parts):
            partial_copy(r, lax.rem(my_part + parts - r, parts)).wait_recv()
        summed = partial_in[0].astype(jnp.float32)
        for p in range(1, parts):
            summed = summed + partial_in[p].astype(jnp.float32)
        gate, up = summed[:, :width], summed[:, width:]
        hidden[my_part] = (gate / (1.0 + jnp.exp(-gate)) * up).astype(jnp.bfloat16)
        for r in range(1, parts):
            hidden_copy(r, my_part).start()

    def make_results():
        for r in range(1, parts):
            hidden_copy(r, lax.rem(my_part + parts - r, parts)).wait_recv()
        down_load.wait()
        product = jnp.dot(
            hidden[...].reshape(owners * group, width),
            down_buf[...],
            preferred_element_type=jnp.float32,
        )
        results = product.astype(jnp.bfloat16).astype(jnp.float32)
        results = results.reshape(owners, group, local_rows)
        for e in range(owners):
            pieces = slots[e, :, pl.ds(local_rows, spare_lanes)].astype(jnp.float32)
            gate = jnp.sum(
                jnp.where(lax.rem(lanes_of, owners) == me, pieces, 0.0), axis=1, keepdims=True
            )
            weighted[e] = gate * results[e]
        for l in range(levels):
            pair_out[l] = weighted[2 * l + 1 - line].astype(jnp.bfloat16)
        pair_copy().start()

    def send_results():
        pair_copy().wait_recv()
        for l in range(levels):
            total_of = weighted[2 * l + line] + pair_in[l].astype(jnp.float32)
            sums[l] = total_of.astype(jnp.bfloat16)
        for d in range(1, levels):
            return_copy(d, level).start()

    def mix_results():
        mixed = weighted[me] + pair_in[level].astype(jnp.float32)
        for d in range(1, levels):
            source = lax.rem(level + levels - d, levels)
            return_copy(d, source).wait_recv()
            mixed = mixed + returned[source].astype(jnp.float32)
        out_tokens[0] = mixed.astype(jnp.bfloat16)

    skew = skews[lanes]
    reach = (levels - 1) * skew

    def step(i, unused):
        @pl.when(i + lead < chunks)
        def _():
            cross_copy(i + lead).start()

        cross_at = i - jnp.minimum(level, levels - 1 - level) * skew

        @pl.when((cross_at >= 0) & (cross_at < chunks))
        def _():
            cross_copy(cross_at).wait_recv()

        up_at = i - level * skew

        def move_up(here):
            @pl.when(here & (up_at >= 0) & (up_at < chunks))
            def _():
                @pl.when(level > 0)
                def _():
                    up_copy(up_at, me).wait_recv()

                @pl.when(level < levels - 1)
                def _():
                    forward(up_at, got_up, stage_up, up_mine, up_other)
                    up_copy(up_at, me + 2).start()

        move_up(level < levels // 2)
        down_at = i - (levels - 1 - level) * skew

        @pl.when((down_at >= 0) & (down_at < chunks))
        def _():
            @pl.when(level < levels - 1)
            def _():
                down_copy(down_at, me).wait_recv()

            @pl.when(level > 0)
            def _():
                forward(down_at, got_down, stage_down, down_mine, down_other)
                down_copy(down_at, me - 2).start()

        move_up(level >= levels // 2)
        at = i - reach

        @pl.when((at >= 0) & (at < chunks))
        def _():
            mine = own[line, rows_of(at), :]
            other = cross[rows_of(at), :]
            keep = jnp.where(origin_mine == 0, mine, other)
            give = jnp.where(origin_other == 0, mine, other)
            for k in range(lanes):
                value = got_up[at, k]
                keep = jnp.where(origin_mine == 2 + k, value, keep)
                give = jnp.where(origin_other == 2 + k, value, give)
                value = got_down[at, k]
                keep = jnp.where(origin_mine == 2 + lanes + k, value, keep)
                give = jnp.where(origin_other == 2 + lanes + k, value, give)
            stage_final[rows_of(at), :] = give
            final_copy(at, line).start()
            final[line, rows_of(at), :] = keep

        landed = i - reach - lag

        @pl.when((landed >= 0) & (landed < chunks))
        def _():
            final_copy(landed, 1 - line).wait_recv()

        @pl.when(i < blocks)
        def _():
            adam_block(i)

        since = i - pass_from

        @pl.when((since >= 0) & (since < levels * pass_every) & (since % pass_every == 0))
        def _():
            pass_tokens(since // pass_every)

        work = (send_partials, send_hidden, make_results, send_results)
        for when, job in zip(token_steps + (chunks + skew + return_step,), work):
            pl.when(i == when)(job)
        return unused

    lax.fori_loop(0, chunks + reach + lag, step, 0)
    mix_results()

    token_swap(me).wait_send()
    for hop in range(levels - 1):

        @pl.when((level - hop >= 0) & (level < levels - 1))
        def _():
            token_copy(hop, level - hop, me, 1).wait_send()

        @pl.when((level + hop < levels) & (level > 0))
        def _():
            token_copy(hop, level + hop, me, 1 + levels).wait_send()

    pair_copy().wait_send()
    for d in range(1, levels):
        return_copy(d, level).wait_send()
    for r in range(1, parts):
        partial_copy(r, my_part).wait_send()
        hidden_copy(r, my_part).wait_send()

    def whole_wait(buffer, sem):
        pltpu.make_async_remote_copy(
            src_ref=buffer, dst_ref=buffer, send_sem=sem, recv_sem=sem, device_id={"expert": partner}
        ).wait_send()

    whole_wait(cross, cross_send)
    whole_wait(stage_final, final_send)

    @pl.when(level < levels - 1)
    def _():
        whole_wait(stage_up, up_send)

    @pl.when(level > 0)
    def _():
        whole_wait(stage_down, down_send)


def write_kernel(tokens, final, out_tokens, new_proj, new_down, sem):
    local_rows, width = new_proj.shape[2:]
    half_width = width // 2
    extra = local_rows - width
    tall = half_width // (width // extra)
    folded = final.shape[1] - local_rows
    copies = [(tokens, out_tokens)]
    for h in (0, 1):
        copies.append((final.at[h, pl.ds(folded, local_rows), :], new_proj.at[0, h]))
        rows = pl.ds(h * half_width, half_width)
        copies.append((final.at[h, pl.ds(0, half_width), :], new_down.at[0, rows, pl.ds(0, width)]))
        for i in range(width // extra):
            rows = pl.ds(h * half_width + i * tall, tall)
            copies.append(
                (
                    final.at[h, pl.ds(half_width, tall), pl.ds(i * extra, extra)],
                    new_down.at[0, rows, pl.ds(width, extra)],
                )
            )
    made = [pltpu.make_async_copy(a, b, sem.at[n]) for n, (a, b) in enumerate(copies)]
    for copy in made:
        copy.start()
    for copy in made:
        copy.wait()


def write_call(tokens, final, weights, down):
    copies = 3 + 2 * (1 + down.shape[1] // (down.shape[2] - down.shape[1]))
    hbm = pl.BlockSpec(memory_space=pl.ANY)
    return pl.pallas_call(
        write_kernel,
        out_shape=[jax.ShapeDtypeStruct(a.shape, a.dtype) for a in (tokens, weights, down)],
        in_specs=[hbm, hbm],
        out_specs=[hbm, hbm, hbm],
        scratch_shapes=[pltpu.SemaphoreType.DMA((copies,))],
        compiler_params=pltpu.CompilerParams(vmem_limit_bytes=2**20),
        cost_estimate=pl.CostEstimate(
            flops=0, bytes_accessed=4 * final.size + 4 * tokens.size, transcendentals=0
        ),
        name="write_results",
    )(tokens, final)


def step_call(lanes, tokens, routes, gates, plan, weights, grads, first, second, down):
    owners, parts = lax.axis_size("expert"), lax.axis_size("dp")
    local_rows, width = weights.shape[2:]
    group = tokens.shape[1]
    folded = (width // 2) * local_rows // width
    total = folded + local_rows
    chunks = total // chunk_rows
    per_part = owners * group // parts
    bf16, f32 = jnp.bfloat16, jnp.float32
    lane_buffer = pltpu.VMEM((chunks, lanes, chunk_rows, width), bf16)
    adam_shape = (adam_buffers, 2, adam_rows, width)
    dma = pltpu.SemaphoreType.DMA
    vmem = pl.BlockSpec(memory_space=pltpu.VMEM)
    hbm = pl.BlockSpec(memory_space=pl.ANY)
    moved = 2 * total * width * 2
    return pl.pallas_call(
        functools.partial(step_kernel, lanes),
        out_shape=(
            jax.ShapeDtypeStruct(tokens.shape, bf16),
            pltpu.VMEM((2, total, width), bf16),
        ),
        in_specs=[pl.BlockSpec(memory_space=pltpu.SMEM), vmem, vmem, vmem] + [hbm] * 5,
        out_specs=(vmem, vmem),
        scratch_shapes=[
            pltpu.VMEM((2, total, width), bf16),
            pltpu.VMEM((total, width), bf16),
            lane_buffer,
            lane_buffer,
            lane_buffer,
            lane_buffer,
            pltpu.VMEM((total, width), bf16),
            pltpu.VMEM(adam_shape, bf16),
            pltpu.VMEM(adam_shape, bf16),
            pltpu.VMEM(adam_shape, f32),
            pltpu.VMEM(adam_shape, f32),
            pltpu.VMEM((width, local_rows), bf16),
            pltpu.VMEM((owners, group, local_rows + 128), bf16),
            pltpu.VMEM((parts, per_part, 2 * width), bf16),
            pltpu.VMEM((parts, per_part, 2 * width), bf16),
            pltpu.VMEM((parts, per_part, width), bf16),
            pltpu.VMEM((owners, group, local_rows), f32),
            pltpu.VMEM((owners // 2, group, local_rows), bf16),
            pltpu.VMEM((owners // 2, group, local_rows), bf16),
            pltpu.VMEM((owners // 2, group, local_rows), bf16),
            pltpu.VMEM((owners // 2, group, local_rows), bf16),
            dma,
            dma,
            dma((4, adam_buffers)),
            dma,
            dma((chunks,)),
            dma,
            dma((chunks,)),
            dma,
            dma((chunks,)),
            dma,
            dma((chunks,)),
            dma((owners + 1,)),
            dma((owners + 1,)),
            dma((parts,)),
            dma((parts,)),
            dma((parts,)),
            dma((parts,)),
            dma,
            dma,
            dma((owners,)),
            dma((owners,)),
        ],
        compiler_params=pltpu.CompilerParams(
            collective_id=lanes, has_side_effects=True, vmem_limit_bytes=vmem_limit[lanes] * 2**20
        ),
        cost_estimate=pl.CostEstimate(
            flops=6 * owners * group * local_rows * width,
            bytes_accessed=6 * moved,
            transcendentals=2 * local_rows * width,
        ),
        name=f"adam_migrate_route_{lanes}",
    )(plan, jnp.swapaxes(routes, 1, 2), jnp.swapaxes(gates, 1, 2), tokens, weights, grads, first, second, down)


def body(
    tokens, routes, gates, plan, proj_weight, proj_grad, first_moment, second_moment, down_weight
):
    args = (tokens, routes, gates, plan, proj_weight, proj_grad, first_moment, second_moment, down_weight)
    owners = lax.axis_size("expert")
    levels = owners // 2
    if levels > max_levels or owners != routes.shape[2] or not foldable(*proj_weight.shape[2:]):
        return generic_body(*args)
    fewest = min(2, levels)
    choices = range(fewest, levels + 1)
    expert_ids = jnp.arange(owners, dtype=jnp.int32)
    crossing = [
        jnp.sum(((expert_ids < 2 * cut) & (plan >= 2 * cut)).astype(jnp.int32))
        for cut in range(2, levels - 1)
    ]
    widest = functools.reduce(jnp.maximum, crossing, jnp.int32(fewest))

    def step_with(lanes):
        return lambda *args: write_call(*step_call(lanes, *args), proj_weight, down_weight)

    return lax.switch(widest - fewest, [step_with(lanes) for lanes in choices], *args)


def solution(mesh):
    in_specs = (
        P("expert", None, "dp"),
        P("expert", None, None),
        P("expert", None, None),
        P(),
        P("expert", None, "dp", None),
        P("expert", None, "dp", None),
        P("expert", None, "dp", None),
        P("expert", None, "dp", None),
        P("expert", None, "dp"),
    )
    out_specs = (P("expert", None, "dp"), P("expert", None, "dp", None), P("expert", None, "dp"))
    return jax.shard_map(body, mesh=mesh, in_specs=in_specs, out_specs=out_specs, check_vma=False)
```

```python
import functools

import jax
import jax.numpy as jnp
from jax import lax
from jax.experimental import pallas as pl
from jax.experimental.pallas import tpu as pltpu
from jax.sharding import PartitionSpec as P

learning_rate = 0.01
beta_first = 0.9
beta_second = 0.999
adam_epsilon = 1e-08
bias_first = 1.0 - 0.9**10
bias_second = 1.0 - 0.999**10

chunk_rows = 16
adam_rows = 64
adam_buffers = 4
skews = {1: 4, 2: 4, 3: 3, 4: 3}
lead = 14
lag = 5
pass_from = 0
pass_every = 3
token_steps = (20, 30, 40)
return_step = 3
max_levels = 4
vmem_limit = {2: 38, 3: 48, 4: 54}


def adam_update(weights, grads, first_moment, second_moment):
    grad_float = grads.astype(jnp.float32)
    first_new = beta_first * first_moment + (1.0 - beta_first) * grad_float
    second_new = beta_second * second_moment + (1.0 - beta_second) * grad_float * grad_float
    adam_step = first_new / bias_first / (jnp.sqrt(second_new / bias_second) + adam_epsilon)
    return (weights.astype(jnp.float32) - learning_rate * adam_step).astype(jnp.bfloat16)


def partial_products(slots, updated):
    joined = jnp.concatenate([updated[0], updated[1]], axis=1)
    return jnp.dot(slots, joined, preferred_element_type=jnp.float32).astype(jnp.bfloat16)


def dp_blocks(partials):
    parts = lax.axis_size("dp")
    return lax.all_to_all(
        partials.reshape(1, parts, -1, partials.shape[1]),
        "dp",
        split_axis=1,
        concat_axis=1,
        tiled=True,
    )


def finish_rows(blocks, down_local):
    width = down_local.shape[0]
    summed = jnp.sum(blocks[0].astype(jnp.float32), axis=0)
    hidden = (jax.nn.silu(summed[:, :width]) * summed[:, width:]).astype(jnp.bfloat16)
    result = jnp.dot(
        lax.all_gather(hidden, "dp", axis=0, tiled=True),
        down_local,
        preferred_element_type=jnp.float32,
    )
    return result.astype(jnp.bfloat16)


def owner_exchange(pieces):
    return lax.all_to_all(pieces, "expert", split_axis=1, concat_axis=1, tiled=True)


def two_phase_migration(plan, updated, down_local):
    owners = lax.axis_size("expert")
    local_rows, width = updated.shape[1:]
    expert_ids = jnp.arange(owners, dtype=jnp.int32)
    spread_down = owner_exchange(down_local.reshape(1, owners, width // owners, local_rows))
    spread_proj = owner_exchange(updated.reshape(2, owners, local_rows // owners, width))
    inverse = jnp.sum(
        jnp.where(plan[None, :] == expert_ids[:, None], expert_ids[None, :], 0), axis=1
    )

    def reordered(blocks):
        return jnp.concatenate(
            [lax.dynamic_slice_in_dim(blocks, inverse[e], 1, axis=1) for e in range(owners)], axis=1
        )

    moved_down = owner_exchange(reordered(spread_down))
    moved_proj = owner_exchange(reordered(spread_proj))
    return moved_proj.reshape(2, local_rows, width), moved_down.reshape(width, local_rows)


def generic_body(
    tokens, routes, gates, plan, proj_weight, proj_grad, first_moment, second_moment, down_weight
):
    owners = lax.axis_size("expert")
    local_rows = proj_weight.shape[2]
    group_tokens = tokens.shape[1]
    route_count = routes.shape[2]
    capacity = min(group_tokens, 3 * group_tokens * route_count // (2 * owners))
    down_local = down_weight[0]
    expert_ids = jnp.arange(owners, dtype=jnp.int32)
    target_match = routes[0][:, :, None] == expert_ids[None, None, :]
    routed = jnp.sum(target_match.astype(jnp.int32), axis=1)
    weighting = jnp.sum(jnp.where(target_match, gates[0][:, :, None], 0.0), axis=1)
    token_ids = jnp.arange(group_tokens, dtype=jnp.int32)
    before = (token_ids[None, :] < token_ids[:, None]).astype(jnp.bfloat16)
    ranks = jnp.dot(
        before, routed.astype(jnp.bfloat16), preferred_element_type=jnp.float32
    ).astype(jnp.int32)
    slot_ids = jnp.arange(capacity, dtype=jnp.int32)
    select = jnp.logical_and(
        ranks.T[:, None, :] == slot_ids[None, :, None], routed.T[:, None, :] > 0
    )
    dispatch_buf = jnp.einsum(
        "ost,td->osd", select.astype(jnp.bfloat16), tokens[0], preferred_element_type=jnp.float32
    ).astype(jnp.bfloat16)
    arrived = owner_exchange(dispatch_buf[None])
    slots = arrived.reshape(owners * capacity, local_rows)
    updated = adam_update(proj_weight[0], proj_grad[0], first_moment[0], second_moment[0])
    new_proj, new_down = two_phase_migration(plan, updated, down_local)
    expert_out = finish_rows(dp_blocks(partial_products(slots, updated)), down_local)
    returned = owner_exchange(expert_out.reshape(1, owners, capacity, local_rows))
    combine = select.astype(jnp.float32) * weighting.T[:, None, :]
    mixed = jnp.einsum(
        "ost,osd->td", combine, returned[0].astype(jnp.float32), precision=lax.Precision.HIGHEST
    )
    return (mixed.astype(jnp.bfloat16)[None], new_proj[None], new_down[None])


def foldable(local_rows, width):
    extra = local_rows - width
    return (
        extra > 0
        and width % extra == 0
        and (width // 2) % (width // extra) == 0
        and local_rows % adam_rows == 0
        and ((width // 2) * local_rows // width) % chunk_rows == 0
    )


def lane_slots(sources, targets, lanes, upward):
    count = len(sources)
    order = range(count) if upward else range(count - 1, -1, -1)
    lane_of, moves, done = {}, {}, []
    for e in order:
        moves[e] = targets[e] > sources[e] if upward else targets[e] < sources[e]
        lane = jnp.int32(0)
        found = jnp.bool_(False)
        for k in range(lanes):
            taken = jnp.bool_(False)
            for p in done:
                if upward:
                    open_still = targets[p] > sources[e]
                else:
                    open_still = targets[p] < sources[e]
                taken = taken | (moves[p] & open_still & (lane_of[p] == k))
            lane = jnp.where(jnp.logical_not(found) & jnp.logical_not(taken), k, lane)
            found = found | jnp.logical_not(taken)
        lane_of[e] = lane
        done.append(e)
    return lane_of, moves


def step_kernel(
    lanes,
    plan,
    routes,
    gates,
    tokens,
    weight_hbm,
    grad_hbm,
    first_hbm,
    second_hbm,
    down_hbm,
    out_tokens,
    final,
    own,
    cross,
    stage_up,
    stage_down,
    got_up,
    got_down,
    stage_final,
    weight_buf,
    grad_buf,
    first_buf,
    second_buf,
    down_buf,
    slots,
    partial_out,
    partial_in,
    hidden,
    weighted,
    pair_out,
    pair_in,
    sums,
    returned,
    fold_sem,
    down_sem,
    adam_sem,
    cross_send,
    cross_recv,
    up_send,
    up_recv,
    down_send,
    down_recv,
    final_send,
    final_recv,
    token_send,
    token_recv,
    partial_send,
    partial_recv,
    hidden_send,
    hidden_recv,
    pair_send,
    pair_recv,
    return_send,
    return_recv,
):
    owners = lax.axis_size("expert")
    parts = lax.axis_size("dp")
    levels = owners // 2
    local_rows, width = weight_hbm.shape[2:]
    half_width = width // 2
    extra = local_rows - width
    strips = width // extra
    tall = half_width // strips
    folded = half_width * local_rows // width
    total = folded + local_rows
    chunks, down_chunks = total // chunk_rows, folded // chunk_rows
    blocks = local_rows // adam_rows
    group = tokens.shape[1]
    per_part = owners * group // parts
    spare_lanes = slots.shape[2] - local_rows
    me, my_part = lax.axis_index("expert"), lax.axis_index("dp")
    level, line = me // 2, me % 2
    partner = 2 * level + 1 - line

    def rows_of(c):
        return pl.ds(pl.multiple_of(c * chunk_rows, chunk_rows), chunk_rows)

    def peer(r):
        return lax.rem(me + r, owners)

    def part_peer(r):
        return lax.rem(my_part + r, parts)

    def fold_copies():
        made = []
        for h in (0, 1):
            made.append(
                pltpu.make_async_copy(
                    down_hbm.at[0, pl.ds(h * half_width, half_width), pl.ds(0, width)],
                    own.at[h, pl.ds(0, half_width), :],
                    fold_sem,
                )
            )
            for i in range(strips):
                made.append(
                    pltpu.make_async_copy(
                        down_hbm.at[0, pl.ds(h * half_width + i * tall, tall), pl.ds(width, extra)],
                        own.at[h, pl.ds(half_width, tall), pl.ds(i * extra, extra)],
                        fold_sem,
                    )
                )
        return made

    def adam_copies(block):
        slot = lax.rem(block, adam_buffers)
        rows = pl.ds(pl.multiple_of(block * adam_rows, adam_rows), adam_rows)
        pairs = (
            (weight_hbm, weight_buf),
            (grad_hbm, grad_buf),
            (first_hbm, first_buf),
            (second_hbm, second_buf),
        )
        return [
            pltpu.make_async_copy(
                source.at[0, :, rows, :], target.at[slot], adam_sem.at[n, slot]
            )
            for n, (source, target) in enumerate(pairs)
        ]

    def cross_copy(c):
        return pltpu.make_async_remote_copy(
            src_ref=own.at[1 - line, rows_of(c), :],
            dst_ref=cross.at[rows_of(c), :],
            send_sem=cross_send,
            recv_sem=cross_recv.at[c],
            device_id={"expert": partner},
        )

    def up_copy(c, target):
        return pltpu.make_async_remote_copy(
            src_ref=stage_up.at[c],
            dst_ref=got_up.at[c],
            send_sem=up_send,
            recv_sem=up_recv.at[c],
            device_id={"expert": target},
        )

    def down_copy(c, target):
        return pltpu.make_async_remote_copy(
            src_ref=stage_down.at[c],
            dst_ref=got_down.at[c],
            send_sem=down_send,
            recv_sem=down_recv.at[c],
            device_id={"expert": target},
        )

    def final_copy(c, h):
        return pltpu.make_async_remote_copy(
            src_ref=stage_final.at[rows_of(c), :],
            dst_ref=final.at[h, rows_of(c), :],
            send_sem=final_send,
            recv_sem=final_recv.at[c],
            device_id={"expert": partner},
        )

    def token_swap(slot):
        return pltpu.make_async_remote_copy(
            src_ref=slots.at[slot],
            dst_ref=slots.at[slot],
            send_sem=token_send.at[0],
            recv_sem=token_recv.at[0],
            device_id={"expert": partner},
        )

    def token_copy(hop, at_level, target, first):
        pair = slots.at[pl.ds(2 * at_level, 2)]
        return pltpu.make_async_remote_copy(
            src_ref=pair,
            dst_ref=pair,
            send_sem=token_send.at[first + hop],
            recv_sem=token_recv.at[first + hop + 1],
            device_id={"expert": target},
        )

    def partial_copy(r, slot):
        return pltpu.make_async_remote_copy(
            src_ref=partial_out.at[part_peer(r)],
            dst_ref=partial_in.at[slot],
            send_sem=partial_send.at[r],
            recv_sem=partial_recv.at[r],
            device_id={"dp": part_peer(r)},
        )

    def hidden_copy(r, slot):
        return pltpu.make_async_remote_copy(
            src_ref=hidden.at[slot],
            dst_ref=hidden.at[slot],
            send_sem=hidden_send.at[r],
            recv_sem=hidden_recv.at[r],
            device_id={"dp": part_peer(r)},
        )

    def pair_copy():
        return pltpu.make_async_remote_copy(
            src_ref=pair_out,
            dst_ref=pair_in,
            send_sem=pair_send,
            recv_sem=pair_recv,
            device_id={"expert": partner},
        )

    def return_copy(d, slot):
        to_level = lax.rem(level + d, levels)
        return pltpu.make_async_remote_copy(
            src_ref=sums.at[to_level],
            dst_ref=returned.at[slot],
            send_sem=return_send.at[d],
            recv_sem=return_recv.at[d],
            device_id={"expert": 2 * to_level + line},
        )

    lanes_of = lax.broadcasted_iota(jnp.int32, (group, spare_lanes), 1)

    def gate_lanes():
        square = (group, group)
        same = lax.broadcasted_iota(jnp.int32, square, 0) == lax.broadcasted_iota(
            jnp.int32, square, 1
        )
        placed = jnp.zeros((group, spare_lanes), jnp.float32)
        for e in range(owners):
            row = jnp.sum(jnp.where(routes[0] == e, gates[0], 0.0), axis=0, keepdims=True)
            rest = jnp.sum(jnp.where(same, row, 0.0), axis=1, keepdims=True)
            for part in range(3):
                piece = rest.astype(jnp.bfloat16).astype(jnp.float32)
                placed = jnp.where(lanes_of == part * owners + e, piece, placed)
                rest = rest - piece
        return placed.astype(jnp.bfloat16)

    for copy in fold_copies():
        copy.start()
    for block in range(adam_buffers):
        for copy in adam_copies(jnp.int32(block)):
            copy.start()
    down_load = pltpu.make_async_copy(down_hbm.at[0], down_buf, down_sem)
    down_load.start()
    slots[me, :, pl.ds(0, local_rows)] = tokens[0]
    slots[me, :, pl.ds(local_rows, spare_lanes)] = gate_lanes()

    barrier = pltpu.get_barrier_semaphore()
    for r in range(1, owners):
        pl.semaphore_signal(barrier, inc=1, device_id={"expert": peer(r)})
    for r in range(1, parts):
        pl.semaphore_signal(barrier, inc=1, device_id={"dp": part_peer(r)})
    pl.semaphore_wait(barrier, owners + parts - 2)

    pltpu.make_async_copy(
        own.at[:, pl.ds(0, folded), :], own.at[:, pl.ds(0, folded), :], fold_sem
    ).wait()
    for c in range(lead):
        cross_copy(c).start()
        if c == 0:
            token_swap(me).start()

    sources = [e // 2 for e in range(owners)]
    targets = [plan[e] // 2 for e in range(owners)]
    up_lane, goes_up = lane_slots(sources, targets, lanes, True)
    down_lane, goes_down = lane_slots(sources, targets, lanes, False)

    def at_me(values):
        mine, other = jnp.int32(-1), jnp.int32(-1)
        for e in range(owners):
            mine = jnp.where(me == e, values[e], mine)
            other = jnp.where(partner == e, values[e], other)
        return mine, other

    up_mine, up_other = at_me([jnp.where(goes_up[e], up_lane[e], -1) for e in range(owners)])
    down_mine, down_other = at_me(
        [jnp.where(goes_down[e], down_lane[e], -1) for e in range(owners)]
    )
    origin_mine, origin_other = jnp.int32(0), jnp.int32(0)
    for e in range(owners):
        origin = jnp.where(
            goes_up[e] & (level != sources[e]),
            2 + up_lane[e],
            jnp.where(
                goes_down[e] & (level != sources[e]),
                2 + lanes + down_lane[e],
                jnp.where(me == e, 0, 1),
            ),
        )
        origin_mine = jnp.where(plan[e] == me, origin, origin_mine)
        origin_other = jnp.where(plan[e] == partner, origin, origin_other)

    def forward(c, got, stage, lane_mine, lane_other):
        mine = own[line, rows_of(c), :]
        other = cross[rows_of(c), :]
        for k in range(lanes):
            value = jnp.where(lane_mine == k, mine, got[c, k])
            stage[c, k] = jnp.where(lane_other == k, other, value)

    def adam_block(i):
        for copy in adam_copies(i):
            copy.wait()
        slot = lax.rem(i, adam_buffers)
        strips_of = adam_rows // 16

        def strip(j, unused):
            h = j // strips_of
            at = pl.multiple_of((j % strips_of) * 16, 16)
            rows = pl.ds(at, 16)
            grad = grad_buf[slot, h, rows, :].astype(jnp.float32)
            first = beta_first * first_buf[slot, h, rows, :] + (1.0 - beta_first) * grad
            second = beta_second * second_buf[slot, h, rows, :] + (1.0 - beta_second) * grad * grad
            scaled = first * (learning_rate / bias_first)
            denominator = jnp.sqrt(second * (1.0 / bias_second)) + adam_epsilon
            value = weight_buf[slot, h, rows, :].astype(jnp.float32) - scaled / denominator
            start = pl.multiple_of(folded + i * adam_rows + at, 16)
            own[h, pl.ds(start, 16), :] = value.astype(jnp.bfloat16)
            return unused

        lax.fori_loop(0, 2 * strips_of, strip, 0)

        @pl.when(i + adam_buffers < blocks)
        def _():
            for copy in adam_copies(i + adam_buffers):
                copy.start()

    def pass_tokens(hop):
        @pl.when(hop == 0)
        def _():
            token_swap(partner).wait_recv()

        for first, from_level, edge, target in (
            (1, level - hop, levels - 1, me + 2),
            (1 + levels, level + hop, 0, me - 2),
        ):

            @pl.when((from_level >= 0) & (from_level < levels))
            def _():
                @pl.when(hop > 0)
                def _():
                    token_copy(hop - 1, from_level, me, first).wait_recv()

                @pl.when(level != edge)
                def _():
                    token_copy(hop, from_level, target, first).start()

    def send_partials():
        gathered = slots[:, :, pl.ds(0, local_rows)].reshape(owners * group, local_rows)
        for h in (0, 1):
            product = jnp.dot(
                gathered, own[h, pl.ds(folded, local_rows), :], preferred_element_type=jnp.float32
            )
            partial_out[:, :, pl.ds(h * width, width)] = product.astype(jnp.bfloat16).reshape(
                parts, per_part, width
            )
        for r in range(1, parts):
            partial_copy(r, my_part).start()
        partial_in[my_part] = partial_out[my_part]

    def send_hidden():
        for r in range(1, parts):
            partial_copy(r, lax.rem(my_part + parts - r, parts)).wait_recv()
        summed = partial_in[0].astype(jnp.float32)
        for p in range(1, parts):
            summed = summed + partial_in[p].astype(jnp.float32)
        gate, up = summed[:, :width], summed[:, width:]
        hidden[my_part] = (gate / (1.0 + jnp.exp(-gate)) * up).astype(jnp.bfloat16)
        for r in range(1, parts):
            hidden_copy(r, my_part).start()

    def make_results():
        for r in range(1, parts):
            hidden_copy(r, lax.rem(my_part + parts - r, parts)).wait_recv()
        down_load.wait()
        product = jnp.dot(
            hidden[...].reshape(owners * group, width),
            down_buf[...],
            preferred_element_type=jnp.float32,
        )
        results = product.astype(jnp.bfloat16).astype(jnp.float32)
        results = results.reshape(owners, group, local_rows)
        for e in range(owners):
            pieces = slots[e, :, pl.ds(local_rows, spare_lanes)].astype(jnp.float32)
            gate = jnp.sum(
                jnp.where(lax.rem(lanes_of, owners) == me, pieces, 0.0), axis=1, keepdims=True
            )
            weighted[e] = gate * results[e]
        for l in range(levels):
            pair_out[l] = weighted[2 * l + 1 - line].astype(jnp.bfloat16)
        pair_copy().start()

    def send_results():
        pair_copy().wait_recv()
        for l in range(levels):
            total_of = weighted[2 * l + line] + pair_in[l].astype(jnp.float32)
            sums[l] = total_of.astype(jnp.bfloat16)
        for d in range(1, levels):
            return_copy(d, level).start()

    def mix_results():
        mixed = weighted[me] + pair_in[level].astype(jnp.float32)
        for d in range(1, levels):
            source = lax.rem(level + levels - d, levels)
            return_copy(d, source).wait_recv()
            mixed = mixed + returned[source].astype(jnp.float32)
        out_tokens[0] = mixed.astype(jnp.bfloat16)

    skew = skews[lanes]
    reach = (levels - 1) * skew

    def step(i, unused):
        cross_at = i - jnp.minimum(level, levels - 1 - level) * skew

        @pl.when((cross_at >= 0) & (cross_at < chunks))
        def _():
            cross_copy(cross_at).wait_recv()

        up_at = i - level * skew

        def move_up(here):
            @pl.when(here & (up_at >= 0) & (up_at < chunks))
            def _():
                @pl.when(level > 0)
                def _():
                    up_copy(up_at, me).wait_recv()

                @pl.when(level < levels - 1)
                def _():
                    forward(up_at, got_up, stage_up, up_mine, up_other)
                    up_copy(up_at, me + 2).start()

        move_up(level < levels // 2)
        down_at = i - (levels - 1 - level) * skew

        @pl.when((down_at >= 0) & (down_at < chunks))
        def _():
            @pl.when(level < levels - 1)
            def _():
                down_copy(down_at, me).wait_recv()

            @pl.when(level > 0)
            def _():
                forward(down_at, got_down, stage_down, down_mine, down_other)
                down_copy(down_at, me - 2).start()

        move_up(level >= levels // 2)

        @pl.when(i + lead < chunks)
        def _():
            cross_copy(i + lead).start()

        at = i - reach

        @pl.when((at >= 0) & (at < chunks))
        def _():
            mine = own[line, rows_of(at), :]
            other = cross[rows_of(at), :]
            keep = jnp.where(origin_mine == 0, mine, other)
            give = jnp.where(origin_other == 0, mine, other)
            for k in range(lanes):
                value = got_up[at, k]
                keep = jnp.where(origin_mine == 2 + k, value, keep)
                give = jnp.where(origin_other == 2 + k, value, give)
                value = got_down[at, k]
                keep = jnp.where(origin_mine == 2 + lanes + k, value, keep)
                give = jnp.where(origin_other == 2 + lanes + k, value, give)
            stage_final[rows_of(at), :] = give
            final_copy(at, line).start()
            final[line, rows_of(at), :] = keep

        landed = i - reach - lag

        @pl.when((landed >= 0) & (landed < chunks))
        def _():
            final_copy(landed, 1 - line).wait_recv()

        @pl.when(i < blocks)
        def _():
            adam_block(i)

        since = i - pass_from

        @pl.when((since >= 0) & (since < levels * pass_every) & (since % pass_every == 0))
        def _():
            pass_tokens(since // pass_every)

        work = (send_partials, send_hidden, make_results, send_results)
        for when, job in zip(token_steps + (chunks + skew + return_step,), work):
            pl.when(i == when)(job)
        return unused

    lax.fori_loop(0, chunks + reach + lag, step, 0)
    mix_results()

    token_swap(me).wait_send()
    for hop in range(levels - 1):

        @pl.when((level - hop >= 0) & (level < levels - 1))
        def _():
            token_copy(hop, level - hop, me, 1).wait_send()

        @pl.when((level + hop < levels) & (level > 0))
        def _():
            token_copy(hop, level + hop, me, 1 + levels).wait_send()

    pair_copy().wait_send()
    for d in range(1, levels):
        return_copy(d, level).wait_send()
    for r in range(1, parts):
        partial_copy(r, my_part).wait_send()
        hidden_copy(r, my_part).wait_send()

    def whole_wait(buffer, sem):
        pltpu.make_async_remote_copy(
            src_ref=buffer, dst_ref=buffer, send_sem=sem, recv_sem=sem, device_id={"expert": partner}
        ).wait_send()

    whole_wait(cross, cross_send)
    whole_wait(stage_final, final_send)

    @pl.when(level < levels - 1)
    def _():
        whole_wait(stage_up, up_send)

    @pl.when(level > 0)
    def _():
        whole_wait(stage_down, down_send)


def write_kernel(tokens, final, out_tokens, new_proj, new_down, sem):
    local_rows, width = new_proj.shape[2:]
    half_width = width // 2
    extra = local_rows - width
    tall = half_width // (width // extra)
    folded = final.shape[1] - local_rows
    copies = [(tokens, out_tokens)]
    for h in (0, 1):
        copies.append((final.at[h, pl.ds(folded, local_rows), :], new_proj.at[0, h]))
        rows = pl.ds(h * half_width, half_width)
        copies.append((final.at[h, pl.ds(0, half_width), :], new_down.at[0, rows, pl.ds(0, width)]))
        for i in range(width // extra):
            rows = pl.ds(h * half_width + i * tall, tall)
            copies.append(
                (
                    final.at[h, pl.ds(half_width, tall), pl.ds(i * extra, extra)],
                    new_down.at[0, rows, pl.ds(width, extra)],
                )
            )
    made = [pltpu.make_async_copy(a, b, sem.at[n]) for n, (a, b) in enumerate(copies)]
    for copy in made:
        copy.start()
    for copy in made:
        copy.wait()


def write_call(tokens, final, weights, down):
    copies = 3 + 2 * (1 + down.shape[1] // (down.shape[2] - down.shape[1]))
    hbm = pl.BlockSpec(memory_space=pl.ANY)
    return pl.pallas_call(
        write_kernel,
        out_shape=[jax.ShapeDtypeStruct(a.shape, a.dtype) for a in (tokens, weights, down)],
        in_specs=[hbm, hbm],
        out_specs=[hbm, hbm, hbm],
        scratch_shapes=[pltpu.SemaphoreType.DMA((copies,))],
        compiler_params=pltpu.CompilerParams(vmem_limit_bytes=2**20),
        cost_estimate=pl.CostEstimate(
            flops=0, bytes_accessed=4 * final.size + 4 * tokens.size, transcendentals=0
        ),
        name="write_results",
    )(tokens, final)


def step_call(lanes, tokens, routes, gates, plan, weights, grads, first, second, down):
    owners, parts = lax.axis_size("expert"), lax.axis_size("dp")
    local_rows, width = weights.shape[2:]
    group = tokens.shape[1]
    folded = (width // 2) * local_rows // width
    total = folded + local_rows
    chunks = total // chunk_rows
    per_part = owners * group // parts
    bf16, f32 = jnp.bfloat16, jnp.float32
    lane_buffer = pltpu.VMEM((chunks, lanes, chunk_rows, width), bf16)
    adam_shape = (adam_buffers, 2, adam_rows, width)
    dma = pltpu.SemaphoreType.DMA
    vmem = pl.BlockSpec(memory_space=pltpu.VMEM)
    hbm = pl.BlockSpec(memory_space=pl.ANY)
    moved = 2 * total * width * 2
    return pl.pallas_call(
        functools.partial(step_kernel, lanes),
        out_shape=(
            jax.ShapeDtypeStruct(tokens.shape, bf16),
            pltpu.VMEM((2, total, width), bf16),
        ),
        in_specs=[pl.BlockSpec(memory_space=pltpu.SMEM), vmem, vmem, vmem] + [hbm] * 5,
        out_specs=(vmem, vmem),
        scratch_shapes=[
            pltpu.VMEM((2, total, width), bf16),
            pltpu.VMEM((total, width), bf16),
            lane_buffer,
            lane_buffer,
            lane_buffer,
            lane_buffer,
            pltpu.VMEM((total, width), bf16),
            pltpu.VMEM(adam_shape, bf16),
            pltpu.VMEM(adam_shape, bf16),
            pltpu.VMEM(adam_shape, f32),
            pltpu.VMEM(adam_shape, f32),
            pltpu.VMEM((width, local_rows), bf16),
            pltpu.VMEM((owners, group, local_rows + 128), bf16),
            pltpu.VMEM((parts, per_part, 2 * width), bf16),
            pltpu.VMEM((parts, per_part, 2 * width), bf16),
            pltpu.VMEM((parts, per_part, width), bf16),
            pltpu.VMEM((owners, group, local_rows), f32),
            pltpu.VMEM((owners // 2, group, local_rows), bf16),
            pltpu.VMEM((owners // 2, group, local_rows), bf16),
            pltpu.VMEM((owners // 2, group, local_rows), bf16),
            pltpu.VMEM((owners // 2, group, local_rows), bf16),
            dma,
            dma,
            dma((4, adam_buffers)),
            dma,
            dma((chunks,)),
            dma,
            dma((chunks,)),
            dma,
            dma((chunks,)),
            dma,
            dma((chunks,)),
            dma((owners + 1,)),
            dma((owners + 1,)),
            dma((parts,)),
            dma((parts,)),
            dma((parts,)),
            dma((parts,)),
            dma,
            dma,
            dma((owners,)),
            dma((owners,)),
        ],
        compiler_params=pltpu.CompilerParams(
            collective_id=lanes, has_side_effects=True, vmem_limit_bytes=vmem_limit[lanes] * 2**20
        ),
        cost_estimate=pl.CostEstimate(
            flops=6 * owners * group * local_rows * width,
            bytes_accessed=6 * moved,
            transcendentals=2 * local_rows * width,
        ),
        name=f"adam_migrate_route_{lanes}",
    )(plan, jnp.swapaxes(routes, 1, 2), jnp.swapaxes(gates, 1, 2), tokens, weights, grads, first, second, down)


def body(
    tokens, routes, gates, plan, proj_weight, proj_grad, first_moment, second_moment, down_weight
):
    args = (tokens, routes, gates, plan, proj_weight, proj_grad, first_moment, second_moment, down_weight)
    owners = lax.axis_size("expert")
    levels = owners // 2
    if levels > max_levels or owners != routes.shape[2] or not foldable(*proj_weight.shape[2:]):
        return generic_body(*args)
    fewest = min(2, levels)
    choices = range(fewest, levels + 1)
    expert_ids = jnp.arange(owners, dtype=jnp.int32)
    crossing = [
        jnp.sum(((expert_ids < 2 * cut) & (plan >= 2 * cut)).astype(jnp.int32))
        for cut in range(2, levels - 1)
    ]
    widest = functools.reduce(jnp.maximum, crossing, jnp.int32(fewest))

    def step_with(lanes):
        return lambda *args: write_call(*step_call(lanes, *args), proj_weight, down_weight)

    return lax.switch(widest - fewest, [step_with(lanes) for lanes in choices], *args)


def solution(mesh):
    in_specs = (
        P("expert", None, "dp"),
        P("expert", None, None),
        P("expert", None, None),
        P(),
        P("expert", None, "dp", None),
        P("expert", None, "dp", None),
        P("expert", None, "dp", None),
        P("expert", None, "dp", None),
        P("expert", None, "dp"),
    )
    out_specs = (P("expert", None, "dp"), P("expert", None, "dp", None), P("expert", None, "dp"))
    return jax.shard_map(body, mesh=mesh, in_specs=in_specs, out_specs=out_specs, check_vma=False)
```
